32 devices in a mesh: seg: 8 (over z, y), sp: 4 (over x, core).
Axes of the slice: x: 2, y: 2, z: 4, core: 2. Of those that a mesh axis runs over, the one named last changes fastest.
Arguments:
- coeffs: float32 [8, 128, 680], P('sp', 'seg'), may hold values from -0.6 to 0.6
- points: float32 [3, 128, 768], P(None, 'seg'), may hold values from -1 to 1
- owner_leaf: int32 [128, 6], P('seg'), may hold values from 0 to 127, as said below
- reaction: float32 [8, 8], replicated, may hold values from -2 to 2
- fit_matrix: float32 [768, 680], replicated, may hold values from -0.21875 to 0.21875
- new_seg: int32 [128], replicated, may hold values from 0 to 7, as said below
- near_src: int32 [128, 16], replicated, may hold values from -1 to 127, as said below
- near_op: int32 [128, 16], replicated, may hold values from 0 to 1
- near_mat: bfloat16 [2, 680, 680], replicated, may hold values from -0.0546875 to 0.0546875
- up_mat: bfloat16 [680, 152], replicated, may hold values from -0.21875 to 0.21875
- far_src: int32 [128, 8], replicated, may hold values from -1 to 127, as said below
- trans_mat: bfloat16 [8, 152, 152], replicated, may hold values from -0.15625 to 0.15625
- down_mat: bfloat16 [152, 680], replicated, may hold values from -0.5 to 0.5
Outputs:
- updated: float32 [8, 192, 680], P('sp', 'seg')
The draws below stay inside these ranges and needn't reach their ends.
Inputs may be any that keep to these rules, and one draw needn't show every extreme that they name: `owner_leaf`: of the 96 blocks of one segment's leaves, at most 24 have their owner among the 16 leaves of any one segment. `new_seg`: never falls along the leaves; leaf t goes to segment t // 16, or to the one before only if t % 16 < 4, or to the one after only if t % 16 >= 12. `near_src`: -1 marks an unused entry; any other entry differs from its row's leaf index by at most 4. `far_src`: -1 marks an absent interaction.
All inputs are finite; a program needn't handle non-finite values.
Results may differ from the reference program's by a relative error of at most 0.0035.
Values may be sent and summed in bfloat16 or wider, within the bound.
A program may use at most 64 MiB of HBM per device.

```python
import jax
import jax.numpy as jnp
import numpy as np
from jax import lax

SPECIES = 8
ORDER = 14
C = 680
Q = 152
NODES = 768
PB = 128
BLOCKS = 6
LEAF_DEV = 16
LEAVES = 128
CAP = 24
MOVE = 4
REACH = 4
MAXL = 24
SLOTS = 192
NEAR = 16
NEAR_OPS = 2
NOPS = 8
N_SEG = 8


def draw_owner_leaf(key, part):
    segment_total = LEAVES // LEAF_DEV
    per_device = LEAF_DEV * BLOCKS
    hot_segment = jax.random.randint(jax.random.fold_in(key, 1), (), 0, segment_total)

    def one_device(device_key):
        spread = jax.random.permutation(jax.random.fold_in(device_key, 2), (segment_total - 1) * CAP)[:per_device - CAP]
        offsets = jnp.concatenate([jnp.zeros((CAP,), jnp.int32), 1 + spread.astype(jnp.int32) // CAP])
        shuffled = offsets[jax.random.permutation(jax.random.fold_in(device_key, 3), per_device)]
        local_leaf = jax.random.randint(jax.random.fold_in(device_key, 4), (per_device,), 0, LEAF_DEV)
        return (hot_segment + shuffled) % segment_total * LEAF_DEV + local_leaf
    device_keys = jax.vmap(lambda device: jax.random.fold_in(key, device + 10))(jnp.arange(segment_total))
    return jax.vmap(one_device)(device_keys).reshape(LEAVES, BLOCKS).astype(jnp.int32)


def draw_new_seg(key, part):
    segment_total = LEAVES // LEAF_DEV
    shifts = jax.random.randint(jax.random.fold_in(key, 1), (segment_total + 1,), -MOVE, MOVE + 1)
    chosen = jax.random.randint(jax.random.fold_in(key, 2), (), 1, segment_total)
    border = jnp.arange(segment_total + 1, dtype=jnp.int32)
    shifts = jnp.where(border == chosen, MOVE, shifts)
    bounds = border * LEAF_DEV + shifts
    bounds = jnp.where(border == 0, 0, jnp.where(border == segment_total, LEAVES, bounds))
    leaf_index = jnp.arange(LEAVES, dtype=jnp.int32)
    home = leaf_index // LEAF_DEV
    later = (leaf_index >= bounds[home]).astype(jnp.int32) + (leaf_index >= bounds[home + 1]).astype(jnp.int32)
    return (home - 1 + later).astype(jnp.int32)


def draw_near_src(key, part):
    leaf_index = jnp.arange(LEAVES, dtype=jnp.int32)[:, None]
    column = jnp.arange(NEAR, dtype=jnp.int32)[None, :]
    offsets = jax.random.randint(jax.random.fold_in(key, 1), (LEAVES, NEAR), -REACH, REACH + 1)
    kept_entry = jax.random.randint(jax.random.fold_in(key, 2), (LEAVES, NEAR), 0, 8) > 0
    special = jax.random.randint(jax.random.fold_in(key, 3), (), 0, LEAVES - REACH)
    forced = (leaf_index == special) & (column == 0)
    offsets = jnp.where(forced, REACH, offsets)
    kept_entry = kept_entry | forced
    source = leaf_index + offsets
    usable = kept_entry & (source >= 0) & (source < LEAVES)
    return jnp.where(usable, source, -1).astype(jnp.int32)


def draw_far_src(key, part):
    source = jax.random.randint(jax.random.fold_in(key, 5), (LEAVES, NOPS), 0, LEAVES)
    kept_entry = jax.random.randint(jax.random.fold_in(key, 6), (LEAVES, NOPS), 0, 8) > 0
    return jnp.where(kept_entry, source, -1).astype(jnp.int32)


def set_ends(drawn, own_key, smallest, largest):
    spot = [jax.random.randint(jax.random.fold_in(own_key, axis), (), 0, length) for axis, length in enumerate(drawn.shape)]
    main_axis = drawn.shape.index(max(drawn.shape))
    next_to = spot[:main_axis] + [(spot[main_axis] + 1) % drawn.shape[main_axis]] + spot[main_axis + 1:]
    return drawn.at[tuple(spot)].set(smallest).at[tuple(next_to)].set(largest)


def block_scale(rng, extent, cuts, low, high):
    def one(axis_at, parts):
        heights = jax.random.uniform(jax.random.fold_in(jax.random.fold_in(rng, 6), axis_at), (parts,), jnp.float32, low / len(cuts), high / len(cuts))
        return jnp.repeat(jnp.exp(heights), extent[axis_at] // parts).reshape((-1,) + (1,) * (len(extent) - axis_at - 1))

    loudness = one(*cuts[0])
    for cut in cuts[1:]:
        loudness = loudness * one(*cut)
    return loudness


def noise(rng, dims, scale, reach, split=(), kind=jnp.bfloat16):
    drawn = jax.random.normal(rng, dims, jnp.float32) * scale
    if len(split) > 0:
        drawn = block_scale(rng, dims, split, -0.22, 0.18) * drawn
    return jnp.clip(drawn, min=-reach, max=reach).astype(kind)


def setup_inputs(seed: int = 0) -> dict:
    arg_keys = jax.random.split(jax.random.key(seed), 14)
    return {
        "coeffs": noise(arg_keys[0], (SPECIES, LEAVES, C), 0.1, 0.6, ((0, 4), (1, 8)), jnp.float32),
        "points": jnp.clip(jax.random.uniform(arg_keys[1], (3, LEAVES, NODES), jnp.float32, -1.0, 1.0) * block_scale(arg_keys[1], (3, LEAVES, NODES), ((1, 8),), -0.4, 0.0), -1.0, 1.0),
        "owner_leaf": draw_owner_leaf(jax.random.fold_in(arg_keys[13], 71), 0),
        "reaction": noise(arg_keys[3], (SPECIES, SPECIES), SPECIES ** -0.5, 2.0, (), jnp.float32),
        "fit_matrix": noise(arg_keys[4], (NODES, C), NODES ** -0.5, 0.21875, (), jnp.float32),
        "new_seg": draw_new_seg(jax.random.fold_in(arg_keys[13], 71), 0),
        "near_src": draw_near_src(jax.random.fold_in(arg_keys[13], 71), 0),
        "near_op": set_ends(jax.random.randint(arg_keys[7], (LEAVES, NEAR), 0, NEAR_OPS), jax.random.fold_in(arg_keys[7], 1), 0, NEAR_OPS - 1).astype(jnp.int32),
        "near_mat": noise(arg_keys[8], (NEAR_OPS, C, C), (C * NEAR) ** -0.5, 0.0546875),
        "up_mat": noise(arg_keys[9], (C, Q), C ** -0.5, 0.21875),
        "far_src": draw_far_src(jax.random.fold_in(arg_keys[13], 71), 0),
        "trans_mat": noise(arg_keys[11], (NOPS, Q, Q), (Q * NOPS) ** -0.5, 0.15625),
        "down_mat": noise(arg_keys[12], (Q, C), Q ** -0.5, 0.5),
    }


precise = lax.Precision.HIGHEST


def basis_tables(order):
    pair_list = [(deg_x, deg_y) for deg_x in range(order + 1) for deg_y in range(order + 1 - deg_x)]
    total_width = (order + 1) * (order + 2) * (order + 3) // 6
    lookup = np.full((len(pair_list), order + 1), total_width, np.int32)
    x_select = np.zeros((len(pair_list), order + 1), np.float32)
    y_select = np.zeros((len(pair_list), order + 1), np.float32)
    counter = 0
    for row_number, (deg_x, deg_y) in enumerate(pair_list):
        x_select[row_number, deg_x] = 1.0
        y_select[row_number, deg_y] = 1.0
        for deg_z in range(order + 1 - deg_x - deg_y):
            lookup[row_number, deg_z] = counter
            counter += 1
    return lookup, x_select, y_select


def chebyshev(position_values, order):
    polynomials = [jnp.ones_like(position_values), position_values]
    for degree in range(2, order + 1):
        polynomials.append(2.0 * position_values * polynomials[-1] - polynomials[-2])
    return jnp.stack(polynomials[: order + 1], axis=-2)


def evaluate(coefficient, coords):
    lookup, x_select, y_select = basis_tables(ORDER)
    padded = jnp.concatenate([coefficient, jnp.zeros(coefficient.shape[:-1] + (1,), coefficient.dtype)], axis=-1)
    dense_coef = jnp.take(padded, jnp.asarray(lookup), axis=-1)
    along_x = chebyshev(coords[0], ORDER)
    along_y = chebyshev(coords[1], ORDER)
    along_z = chebyshev(coords[2], ORDER)
    inner_sum = jnp.einsum('sqk,kp->sqp', dense_coef, along_z, precision=precise)
    y_rows = jnp.einsum('qk,kp->qp', jnp.asarray(y_select, coefficient.dtype), along_y, precision=precise)
    folded = jnp.einsum('sqp,qk->skp', inner_sum * y_rows[None], jnp.asarray(x_select, coefficient.dtype), precision=precise)
    return jnp.sum(folded * along_x[None], axis=1)


def reference(coeffs, points, owner_leaf, reaction, fit_matrix, new_seg, near_src, near_op, near_mat, up_mat, far_src, trans_mat, down_mat):
    coords = points.reshape(3, LEAVES * BLOCKS, PB).transpose(1, 0, 2)
    flat_owner = owner_leaf.reshape(-1).astype(jnp.int32)

    def per_block(block_args):
        coefficient = jnp.take(coeffs, block_args[0], axis=1)
        return evaluate(coefficient, block_args[1])

    values = lax.map(per_block, (flat_owner, coords), batch_size=64)
    values = values.reshape(LEAVES, BLOCKS, SPECIES, PB).transpose(2, 0, 1, 3).reshape(SPECIES, LEAVES, NODES)
    mixing = jnp.einsum('sr,rln->sln', reaction, values, precision=precise)
    reacted = values + jnp.tanh(mixing)
    refitted = jnp.einsum('sln,nc->slc', reacted, fit_matrix, precision=precise)
    ghosts = lax.optimization_barrier(refitted.astype(jnp.bfloat16))
    ghost_wide = ghosts.astype(jnp.float32)
    equivalent = jnp.einsum('slc,cq->slq', ghost_wide, up_mat.astype(jnp.float32), precision=precise).astype(jnp.bfloat16)
    equiv_wide = lax.optimization_barrier(equivalent).astype(jnp.float32)
    near_wide = near_mat.astype(jnp.float32)
    trans_wide = trans_mat.astype(jnp.float32)
    down_wide = down_mat.astype(jnp.float32)

    def per_segment(segment):
        target = segment * LEAF_DEV - MOVE + jnp.arange(MAXL, dtype=jnp.int32)
        inside = (target >= 0) & (target < LEAVES)
        clipped = jnp.clip(target, 0, LEAVES - 1).astype(jnp.int32)
        live_slot = inside & (new_seg[clipped] == segment)
        own_term = jnp.take(ghost_wide, clipped, axis=1)
        near_from = near_src[clipped]
        near_kind = near_op[clipped]
        near_ok = live_slot[:, None] & (near_from >= 0)
        picked = jnp.take(ghost_wide, jnp.clip(near_from, 0, LEAVES - 1).reshape(-1).astype(jnp.int32), axis=1)
        picked = picked.reshape(SPECIES, MAXL, NEAR, C)
        near_term = jnp.zeros((SPECIES, MAXL, C), jnp.float32)
        for operator in range(NEAR_OPS):
            weight_mask = (near_ok & (near_kind == operator)).astype(picked.dtype)
            grouped = jnp.sum(picked * weight_mask[None, :, :, None], axis=2)
            near_term = near_term + jnp.einsum('sjc,cd->sjd', grouped, near_wide[operator], precision=precise)
        far_from = far_src[clipped]
        far_ok = (live_slot[:, None] & (far_from >= 0)).astype(equiv_wide.dtype)
        far_rows = jnp.take(equiv_wide, jnp.clip(far_from, 0, LEAVES - 1).reshape(-1).astype(jnp.int32), axis=1)
        far_rows = far_rows.reshape(SPECIES, MAXL, NOPS, Q) * far_ok[None, :, :, None]
        local_expansion = jnp.einsum('sjoq,oqr->sjr', far_rows, trans_wide, precision=precise).astype(jnp.bfloat16)
        local_expansion = lax.optimization_barrier(local_expansion).astype(jnp.float32)
        far_term = jnp.einsum('sjq,qc->sjc', local_expansion, down_wide, precision=precise)
        total = own_term + near_term + far_term
        return jnp.where(live_slot[None, :, None], total, jnp.zeros_like(total))

    updated = lax.map(per_segment, jnp.arange(N_SEG, dtype=jnp.int32))
    return updated.transpose(1, 0, 2, 3).reshape(SPECIES, SLOTS, C)
```

```python
import functools

import jax
import jax.numpy as jnp
import numpy as np
from jax import lax
from jax.experimental import pallas as pl
from jax.experimental.pallas import tpu as pltpu
from jax.sharding import PartitionSpec as P

ORDER = 14
PB = 128
MOVE = 4
REACH = 4
MESH = pl.DeviceIdType.MESH
VMEM = pl.BlockSpec(memory_space=pltpu.VMEM)
SMEM = pl.BlockSpec(memory_space=pltpu.SMEM)
ANY = pl.BlockSpec(memory_space=pl.ANY)
LIMIT = 60 * 1024 * 1024


def run_starts():
    starts, counter = {}, 0
    for i in range(ORDER + 1):
        for j in range(ORDER + 1 - i):
            starts[i, j] = counter
            counter += ORDER + 1 - i - j
    return starts, counter


GROUPS = [(i, 0) for i in range(ORDER + 1)] + [(i, 1) for i in range(ORDER + 1 - 8)]
ROWS = 8 * len(GROUPS)


def remote(src, dst, send, recv, axis, to):
    return pltpu.make_async_remote_copy(
        src_ref=src, dst_ref=dst, send_sem=send, recv_sem=recv,
        device_id={axis: to}, device_id_type=MESH,
    )


def greet(axis, others):
    barrier = pltpu.get_barrier_semaphore()
    for to in others:
        pl.semaphore_signal(barrier, inc=1, device_id={axis: to}, device_id_type=MESH)
    pl.semaphore_wait(barrier, len(others))


def pair_gather_kernel(axis, n, src, out, send, recv, local):
    me = lax.axis_index(axis)
    half = n // 2
    partner = me + 1 - 2 * lax.rem(me, 2)
    ahead = [lax.rem(me + 2 * p, n) for p in range(half)]
    behind = [lax.rem(me + n - 2 * p, n) for p in range(half)]
    partner_behind = [lax.rem(partner + n - 2 * p, n) for p in range(half)]
    greet(axis, ahead[1:] + [partner])
    own = pltpu.make_async_copy(src, out.at[me], local)
    own.start()
    copies = []
    for p in range(1, half):
        copies.append(remote(src, out.at[me], send.at[p], recv.at[p], axis, ahead[p]))
        copies[-1].start()
    copies.append(remote(src, out.at[me], send.at[half], recv.at[half], axis, partner))
    copies[-1].start()
    for p in range(1, half):
        slot = out.at[behind[p]]
        remote(slot, slot, send.at[p], recv.at[p], axis, partner).wait_recv()
        copies.append(remote(slot, slot, send.at[half + p], recv.at[half + p], axis, partner))
        copies[-1].start()
    for p in range(half):
        slot = out.at[partner_behind[p]]
        remote(slot, slot, send.at[half + p], recv.at[half + p], axis, partner).wait_recv()
    for copy in copies:
        copy.wait_send()
    own.wait()


def pair_gather(value, axis, collective_id):
    n = lax.axis_size(axis)
    return pl.pallas_call(
        functools.partial(pair_gather_kernel, axis, n),
        out_shape=jax.ShapeDtypeStruct((n,) + value.shape, value.dtype),
        in_specs=[ANY],
        out_specs=ANY,
        scratch_shapes=[
            pltpu.SemaphoreType.DMA((n,)),
            pltpu.SemaphoreType.DMA((n,)),
            pltpu.SemaphoreType.DMA,
        ],
        compiler_params=pltpu.CompilerParams(
            collective_id=collective_id, has_side_effects=True
        ),
        name="gather_" + axis,
    )(value)


def evaluate_kernel(owner, coef, points, values, rows, dense, cheb):
    leaf_dev, blocks = owner.shape
    species = values.shape[0]
    width = coef.shape[2]
    starts, _ = run_starts()
    chunk = 8 // species
    for axis in range(3):
        for m in range(blocks):
            for h in range(leaf_dev // 8):
                x = points[axis, 8 * h : 8 * h + 8, PB * m : PB * m + PB]
                first = 16 * (m * leaf_dev + 8 * h)
                below, here = jnp.ones_like(x), x
                cheb[axis, pl.ds(first, 8, stride=16), :] = below
                for d in range(1, ORDER + 1):
                    cheb[axis, pl.ds(first + d, 8, stride=16), :] = here
                    below, here = here, 2.0 * x * here - below
                cheb[axis, pl.ds(first + ORDER + 1, 8, stride=16), :] = jnp.zeros_like(x)
    lane = lax.broadcasted_iota(jnp.int32, (8, 128), 1)

    def expand(c, carry):
        for k in range(chunk):
            b = c * chunk + k
            leaf = owner[lax.rem(b, leaf_dev), lax.div(b, leaf_dev)]
            rows[species * k : species * (k + 1), :width] = coef[leaf]
        tiles = []
        for t in range(rows.shape[1] // 128):
            x = rows[:, 128 * t : 128 * t + 128]
            x_high = x.astype(jnp.bfloat16).astype(jnp.float32)
            tiles.append((x_high, x - x_high))
        zero = jnp.zeros((8, 128), jnp.float32)
        for g, (i, upper) in enumerate(GROUPS):
            for k in range(8):
                j = 8 * upper + k
                if i + j > ORDER:
                    piece = zero
                else:
                    length = ORDER + 1 - i - j
                    t, shift = divmod(starts[i, j], 128)
                    parts = []
                    for kind in range(2):
                        turn = (128 - shift + 16 * kind) % 128
                        part = tiles[t][kind]
                        if turn:
                            part = pltpu.roll(part, turn, 1)
                        if shift + length > 128:
                            rest = pltpu.roll(tiles[t + 1][kind], turn, 1)
                            part = jnp.where(lane < 128 - shift + 16 * kind, part, rest)
                        parts.append(part)
                    second = jnp.where((lane >= 16) & (lane < 16 + length), parts[1], zero)
                    piece = jnp.where(lane < length, parts[0], second)
                dense[pl.ds(c * (8 * ROWS) + 8 * g + k, 8, stride=ROWS), :] = piece
        return carry

    lax.fori_loop(0, leaf_dev * blocks // chunk, expand, 0)

    def block(b):
        lhs = dense[pl.ds(b * (species * ROWS), species * ROWS), 0:32].astype(jnp.bfloat16)
        tx = cheb[0, pl.ds(b * 16, 16), :]
        ty = cheb[1, pl.ds(b * 16, 16), :]
        tz = cheb[2, pl.ds(b * 16, 16), :]
        high = tz.astype(jnp.bfloat16)
        tz_high = high.astype(jnp.float32)
        rhs = jnp.concatenate(
            [
                jnp.concatenate([tz_high, tz - tz_high], axis=1),
                jnp.concatenate([tz_high, jnp.zeros_like(tz)], axis=1),
            ],
            axis=0,
        ).astype(jnp.bfloat16)
        both = jnp.dot(lhs, rhs, preferred_element_type=jnp.float32)
        inner = both[:, :PB] + both[:, PB:]
        for s in range(species):
            total = [None, None]
            for g, (i, upper) in enumerate(GROUPS):
                r = s * ROWS + 8 * g
                term = inner[r : r + 8] * tx[i : i + 1]
                total[upper] = term if total[upper] is None else total[upper] + term
            summed = total[0] * ty[0:8] + total[1] * ty[8:16]
            values[s, pl.ds(b, 1), :] = jnp.sum(summed, axis=0, keepdims=True)

    def pair(c, carry):
        for k in range(4):
            block(4 * c + k)
        return carry

    lax.fori_loop(0, leaf_dev * blocks // 4, pair, 0)


def split(x):
    high = x.astype(jnp.bfloat16)
    return high, (x - high.astype(jnp.float32)).astype(jnp.bfloat16)


def refit_kernel(reaction, own, gathered, fit, up, ghosts, equivalent, reacted):
    species, block_count, _ = own.shape
    leaf_dev = equivalent.shape[0] // species
    blocks = block_count // leaf_dev
    total_species = reaction.shape[1]
    start = lax.axis_index("sp") * species
    for s in range(species):
        mixing = jnp.zeros((block_count, PB), jnp.float32)
        for r in range(total_species):
            other = gathered[r // species, r % species].astype(jnp.float32)
            mixing = mixing + reaction[start + s, r] * other
        result = own[s] + jnp.tanh(mixing)
        for m in range(blocks):
            reacted[s * leaf_dev : (s + 1) * leaf_dev, m * PB : (m + 1) * PB] = result[
                m * leaf_dev : (m + 1) * leaf_dev
            ]
    high, low = split(reacted[...])
    fit_high, fit_low = split(fit[...])
    main = jnp.dot(
        jnp.concatenate([high, low], axis=0), fit_high, preferred_element_type=jnp.float32
    )
    rest = jnp.dot(high, fit_low, preferred_element_type=jnp.float32)
    count = species * leaf_dev
    refitted = main[:count] + (main[count:] + rest)
    rounded = refitted.astype(jnp.bfloat16)
    half = leaf_dev // 2
    for s in range(species):
        for h in range(2):
            first = s * leaf_dev + h * half
            ghosts[h, s] = refitted[first : first + half].astype(jnp.bfloat16)
    equivalent[...] = jnp.dot(
        rounded, up[...], preferred_element_type=jnp.float32
    ).astype(jnp.bfloat16)


def exchange_kernel(n, ghosts, equivalent, before, after, everyone, send, recv, local):
    me = lax.axis_index("seg")
    ahead = [lax.rem(me + p, n) for p in range(n)]
    behind = [lax.rem(me + n - p, n) for p in range(n)]
    greet("seg", ahead[1:])
    own = pltpu.make_async_copy(equivalent, everyone.at[me], local)
    own.start()
    up = remote(ghosts.at[1], before, send.at[0], recv.at[0], "seg", ahead[1])
    down = remote(ghosts.at[0], after, send.at[n], recv.at[n], "seg", behind[1])
    up.start()
    down.start()
    copies = []
    for p in range(1, n):
        copies.append(
            remote(equivalent, everyone.at[me], send.at[p], recv.at[p], "seg", ahead[p])
        )
        copies[-1].start()
    for p in range(1, n):
        slot = everyone.at[behind[p]]
        remote(slot, slot, send.at[p], recv.at[p], "seg", ahead[p]).wait_recv()
    for copy in copies:
        copy.wait_send()
    up.wait()
    down.wait()
    own.wait()


def finish_kernel(
    table, ghosts, before, after, everyone, near_mat, trans, down, out, near_count, far_count
):
    species, slots, width = out.shape
    half = ghosts.shape[2]
    leaf_dev = 2 * half
    me = lax.axis_index("seg")
    n = everyone.shape[0]
    margin = MOVE + REACH
    near_ops = near_mat.shape[0]
    far_ops = trans.shape[0]
    rows = table[pl.ds(pl.multiple_of(me * leaf_dev, 8), slots), :]
    live = rows[:, 0:1] == me
    base = me * leaf_dev - margin
    seen = leaf_dev + 2 * margin
    near_lane = lax.broadcasted_iota(jnp.int32, (slots, seen), 1)
    slot_row = lax.broadcasted_iota(jnp.int32, (slots, seen), 0)
    near_from = rows[:, 1 : 1 + near_count]
    near_kind = rows[:, 1 + near_count : 1 + 2 * near_count]
    far_from = rows[:, 1 + 2 * near_count : 1 + 2 * near_count + far_count]
    near_from = jnp.where(live & (near_from >= 0), near_from - base, -1)
    far_from = jnp.where(live & (far_from >= 0), far_from, -1)
    weights = [((near_lane == slot_row + REACH) & live).astype(jnp.float32)]
    weights += [jnp.zeros((slots, seen), jnp.float32) for _ in range(near_ops)]
    for q in range(near_count):
        hit = near_lane == near_from[:, q : q + 1]
        for o in range(near_ops):
            chosen = hit & (near_kind[:, q : q + 1] == o)
            weights[1 + o] = weights[1 + o] + chosen.astype(jnp.float32)
    weights = jnp.concatenate(weights, axis=0).astype(jnp.bfloat16)
    leaf_total = n * leaf_dev
    far_lane = lax.broadcasted_iota(jnp.int32, (slots, leaf_total), 1)
    picks = jnp.concatenate(
        [(far_lane == far_from[:, o : o + 1]).astype(jnp.float32) for o in range(far_ops)],
        axis=0,
    ).astype(jnp.bfloat16)
    own_term, highs, lows, far_rows = [], [], [], []
    for s in range(species):
        nearby = jnp.concatenate(
            [x.astype(jnp.float32) for x in (before[s], ghosts[0, s], ghosts[1, s], after[s])],
            axis=0,
        ).astype(jnp.bfloat16)
        grouped = jnp.dot(weights, nearby, preferred_element_type=jnp.float32)
        own_term.append(grouped[:slots])
        high, low = split(grouped[slots:])
        highs.append(high)
        lows.append(low)
        source = jnp.concatenate(
            [everyone[e, s * leaf_dev : (s + 1) * leaf_dev, :] for e in range(n)], axis=0
        )
        far_rows.append(
            jnp.dot(picks, source, preferred_element_type=jnp.float32)
        )
    total = jnp.concatenate(own_term, axis=0)
    for o in range(near_ops):
        part = slice(o * slots, (o + 1) * slots)
        stacked = jnp.concatenate(
            [x[part].astype(jnp.float32) for x in highs + lows], axis=0
        ).astype(jnp.bfloat16)
        product = jnp.dot(stacked, near_mat[o], preferred_element_type=jnp.float32)
        total = total + (product[: species * slots] + product[species * slots :])
    expansion = jnp.zeros((species * slots, trans.shape[2]), jnp.float32)
    for o in range(far_ops):
        rows_o = jnp.concatenate(
            [x[o * slots : (o + 1) * slots] for x in far_rows], axis=0
        ).astype(jnp.bfloat16)
        expansion = expansion + jnp.dot(rows_o, trans[o], preferred_element_type=jnp.float32)
    total = total + jnp.dot(
        expansion.astype(jnp.bfloat16), down[...], preferred_element_type=jnp.float32
    )
    for s in range(species):
        out[s] = jnp.where(live, total[s * slots : (s + 1) * slots], 0.0)


def shards(
    coeffs, points, owner_leaf, reaction, fit_matrix, new_seg, near_src, near_op,
    near_mat, up_mat, far_src, trans_mat, down_mat,
):
    species, leaf_dev, width = coeffs.shape
    n = lax.axis_size("seg")
    blocks = owner_leaf.shape[1]
    count = leaf_dev * blocks
    padded_width = -(-width // 128) * 128
    slots = leaf_dev + 2 * MOVE
    table = jnp.concatenate([new_seg[:, None], near_src, near_op, far_src], axis=1)
    table = jnp.pad(table, ((MOVE, MOVE), (0, 0)), constant_values=-1)
    mine = jnp.transpose(coeffs, (1, 0, 2))
    everyone = pair_gather(mine, "seg", 0).reshape(n * leaf_dev, species, width)
    values = pl.pallas_call(
        evaluate_kernel,
        out_shape=jax.ShapeDtypeStruct((species, count, PB), jnp.float32),
        in_specs=[SMEM, VMEM, VMEM],
        out_specs=VMEM,
        scratch_shapes=[
            pltpu.VMEM((8, padded_width), jnp.float32),
            pltpu.VMEM((count * species * ROWS, 128), jnp.float32),
            pltpu.VMEM((3, 16 * count, PB), jnp.float32),
        ],
        compiler_params=pltpu.CompilerParams(vmem_limit_bytes=LIMIT),
        name="evaluate",
    )(owner_leaf, everyone, points)
    gathered = pair_gather(values, "sp", 1)
    half = leaf_dev // 2
    ghosts, equivalent = pl.pallas_call(
        refit_kernel,
        out_shape=(
            jax.ShapeDtypeStruct((2, species, half, width), jnp.bfloat16),
            jax.ShapeDtypeStruct((species * leaf_dev, up_mat.shape[1]), jnp.bfloat16),
        ),
        in_specs=[SMEM, VMEM, VMEM, VMEM, VMEM],
        out_specs=(VMEM, VMEM),
        scratch_shapes=[pltpu.VMEM((species * leaf_dev, blocks * PB), jnp.float32)],
        compiler_params=pltpu.CompilerParams(vmem_limit_bytes=LIMIT),
        name="refit",
    )(reaction, values, gathered, fit_matrix, up_mat)
    before, after, all_equivalent = pl.pallas_call(
        functools.partial(exchange_kernel, n),
        out_shape=(
            jax.ShapeDtypeStruct((species, half, width), jnp.bfloat16),
            jax.ShapeDtypeStruct((species, half, width), jnp.bfloat16),
            jax.ShapeDtypeStruct((n,) + equivalent.shape, jnp.bfloat16),
        ),
        in_specs=[ANY, ANY],
        out_specs=(ANY, ANY, ANY),
        scratch_shapes=[
            pltpu.SemaphoreType.DMA((n + 1,)),
            pltpu.SemaphoreType.DMA((n + 1,)),
            pltpu.SemaphoreType.DMA,
        ],
        compiler_params=pltpu.CompilerParams(collective_id=2, has_side_effects=True),
        name="exchange",
    )(ghosts, equivalent)
    return pl.pallas_call(
        functools.partial(
            finish_kernel, near_count=near_src.shape[1], far_count=far_src.shape[1]
        ),
        out_shape=jax.ShapeDtypeStruct((species, slots, width), jnp.float32),
        in_specs=[VMEM] * 8,
        out_specs=VMEM,
        compiler_params=pltpu.CompilerParams(vmem_limit_bytes=LIMIT),
        name="finish",
    )(table, ghosts, before, after, all_equivalent, near_mat, trans_mat, down_mat)


def solution(mesh):
    placed = (P("sp", "seg", None), P(None, "seg", None), P("seg", None)) + (P(),) * 10
    return jax.shard_map(
        shards, mesh=mesh, in_specs=placed, out_specs=P("sp", "seg", None), check_vma=False
    )
```

```python
import functools

import jax
import jax.numpy as jnp
import numpy as np
from jax import lax
from jax.experimental import pallas as pl
from jax.experimental.pallas import tpu as pltpu
from jax.sharding import PartitionSpec as P

ORDER = 14
PB = 128
MOVE = 4
REACH = 4
MESH = pl.DeviceIdType.MESH
VMEM = pl.BlockSpec(memory_space=pltpu.VMEM)
SMEM = pl.BlockSpec(memory_space=pltpu.SMEM)
ANY = pl.BlockSpec(memory_space=pl.ANY)
LIMIT = 60 * 1024 * 1024


def run_starts():
    starts, counter = {}, 0
    for i in range(ORDER + 1):
        for j in range(ORDER + 1 - i):
            starts[i, j] = counter
            counter += ORDER + 1 - i - j
    return starts, counter


GROUPS = [(i, 0) for i in range(ORDER + 1)] + [(i, 1) for i in range(ORDER + 1 - 8)]
ROWS = 8 * len(GROUPS)


def remote(src, dst, send, recv, axis, to):
    return pltpu.make_async_remote_copy(
        src_ref=src, dst_ref=dst, send_sem=send, recv_sem=recv,
        device_id={axis: to}, device_id_type=MESH,
    )


def greet(axis, others):
    barrier = pltpu.get_barrier_semaphore()
    for to in others:
        pl.semaphore_signal(barrier, inc=1, device_id={axis: to}, device_id_type=MESH)
    pl.semaphore_wait(barrier, len(others))


def pair_gather_kernel(axis, n, src, out, send, recv, local):
    me = lax.axis_index(axis)
    half = n // 2
    partner = me + 1 - 2 * lax.rem(me, 2)
    ahead = [lax.rem(me + 2 * p, n) for p in range(half)]
    behind = [lax.rem(me + n - 2 * p, n) for p in range(half)]
    partner_behind = [lax.rem(partner + n - 2 * p, n) for p in range(half)]
    greet(axis, ahead[1:] + [partner])
    own = pltpu.make_async_copy(src, out.at[me], local)
    own.start()
    copies = []
    for p in range(1, half):
        copies.append(remote(src, out.at[me], send.at[p], recv.at[p], axis, ahead[p]))
        copies[-1].start()
    copies.append(remote(src, out.at[me], send.at[half], recv.at[half], axis, partner))
    copies[-1].start()
    for p in range(1, half):
        slot = out.at[behind[p]]
        remote(slot, slot, send.at[p], recv.at[p], axis, partner).wait_recv()
        copies.append(remote(slot, slot, send.at[half + p], recv.at[half + p], axis, partner))
        copies[-1].start()
    for p in range(half):
        slot = out.at[partner_behind[p]]
        remote(slot, slot, send.at[half + p], recv.at[half + p], axis, partner).wait_recv()
    for copy in copies:
        copy.wait_send()
    own.wait()


def pair_gather(value, axis, collective_id):
    n = lax.axis_size(axis)
    return pl.pallas_call(
        functools.partial(pair_gather_kernel, axis, n),
        out_shape=jax.ShapeDtypeStruct((n,) + value.shape, value.dtype),
        in_specs=[ANY],
        out_specs=ANY,
        scratch_shapes=[
            pltpu.SemaphoreType.DMA((n,)),
            pltpu.SemaphoreType.DMA((n,)),
            pltpu.SemaphoreType.DMA,
        ],
        compiler_params=pltpu.CompilerParams(
            collective_id=collective_id, has_side_effects=True
        ),
        name="gather_" + axis,
    )(value)


def evaluate_kernel(owner, coef, points, values, rows, dense, cheb):
    leaf_dev, blocks = owner.shape
    species = values.shape[0]
    width = coef.shape[2]
    starts, _ = run_starts()
    chunk = 8 // species
    for axis in range(3):
        for m in range(blocks):
            for h in range(leaf_dev // 8):
                x = points[axis, 8 * h : 8 * h + 8, PB * m : PB * m + PB]
                first = 16 * (m * leaf_dev + 8 * h)
                below, here = jnp.ones_like(x), x
                cheb[axis, pl.ds(first, 8, stride=16), :] = below
                for d in range(1, ORDER + 1):
                    cheb[axis, pl.ds(first + d, 8, stride=16), :] = here
                    below, here = here, 2.0 * x * here - below
                cheb[axis, pl.ds(first + ORDER + 1, 8, stride=16), :] = jnp.zeros_like(x)
    lane = lax.broadcasted_iota(jnp.int32, (8, 128), 1)

    def expand(c, carry):
        for k in range(chunk):
            b = c * chunk + k
            leaf = owner[lax.rem(b, leaf_dev), lax.div(b, leaf_dev)]
            rows[species * k : species * (k + 1), :width] = coef[leaf]
        tiles = []
        for t in range(rows.shape[1] // 128):
            x = rows[:, 128 * t : 128 * t + 128]
            x_high = x.astype(jnp.bfloat16).astype(jnp.float32)
            tiles.append((x_high, x - x_high))
        zero = jnp.zeros((8, 128), jnp.float32)
        for g, (i, upper) in enumerate(GROUPS):
            for k in range(8):
                j = 8 * upper + k
                if i + j > ORDER:
                    piece = zero
                else:
                    length = ORDER + 1 - i - j
                    t, shift = divmod(starts[i, j], 128)
                    parts = []
                    for kind in range(2):
                        turn = (128 - shift + 16 * kind) % 128
                        part = tiles[t][kind]
                        if turn:
                            part = pltpu.roll(part, turn, 1)
                        if shift + length > 128:
                            rest = pltpu.roll(tiles[t + 1][kind], turn, 1)
                            part = jnp.where(lane < 128 - shift + 16 * kind, part, rest)
                        parts.append(part)
                    second = jnp.where((lane >= 16) & (lane < 16 + length), parts[1], zero)
                    piece = jnp.where(lane < length, parts[0], second)
                dense[pl.ds(c * (8 * ROWS) + 8 * g + k, 8, stride=ROWS), :] = piece
        return carry

    lax.fori_loop(0, leaf_dev * blocks // chunk, expand, 0)

    def block(b):
        lhs = dense[pl.ds(b * (species * ROWS), species * ROWS), 0:32].astype(jnp.bfloat16)
        tx = cheb[0, pl.ds(b * 16, 16), :]
        ty = cheb[1, pl.ds(b * 16, 16), :]
        tz = cheb[2, pl.ds(b * 16, 16), :]
        high = tz.astype(jnp.bfloat16)
        tz_high = high.astype(jnp.float32)
        rhs = jnp.concatenate(
            [
                jnp.concatenate([tz_high, tz - tz_high], axis=1),
                jnp.concatenate([tz_high, jnp.zeros_like(tz)], axis=1),
            ],
            axis=0,
        ).astype(jnp.bfloat16)
        both = jnp.dot(lhs, rhs, preferred_element_type=jnp.float32)
        inner = both[:, :PB] + both[:, PB:]
        for s in range(species):
            total = [None, None]
            for g, (i, upper) in enumerate(GROUPS):
                r = s * ROWS + 8 * g
                term = inner[r : r + 8] * tx[i : i + 1]
                total[upper] = term if total[upper] is None else total[upper] + term
            summed = total[0] * ty[0:8] + total[1] * ty[8:16]
            values[s, pl.ds(b, 1), :] = jnp.sum(summed, axis=0, keepdims=True)

    def pair(c, carry):
        for k in range(4):
            block(4 * c + k)
        return carry

    lax.fori_loop(0, leaf_dev * blocks // 4, pair, 0)


def split(x):
    high = x.astype(jnp.bfloat16)
    return high, (x - high.astype(jnp.float32)).astype(jnp.bfloat16)


def refit_kernel(reaction, own, gathered, fit, up, ghosts, equivalent, reacted):
    species, block_count, _ = own.shape
    leaf_dev = equivalent.shape[0] // species
    blocks = block_count // leaf_dev
    total_species = reaction.shape[1]
    start = lax.axis_index("sp") * species
    for s in range(species):
        mixing = jnp.zeros((block_count, PB), jnp.float32)
        for r in range(total_species):
            other = gathered[r // species, r % species].astype(jnp.float32)
            mixing = mixing + reaction[start + s, r] * other
        result = own[s] + jnp.tanh(mixing)
        for m in range(blocks):
            reacted[s * leaf_dev : (s + 1) * leaf_dev, m * PB : (m + 1) * PB] = result[
                m * leaf_dev : (m + 1) * leaf_dev
            ]
    high, low = split(reacted[...])
    fit_high, fit_low = split(fit[...])
    main = jnp.dot(
        jnp.concatenate([high, low], axis=0), fit_high, preferred_element_type=jnp.float32
    )
    rest = jnp.dot(high, fit_low, preferred_element_type=jnp.float32)
    count = species * leaf_dev
    refitted = main[:count] + (main[count:] + rest)
    rounded = refitted.astype(jnp.bfloat16)
    half = leaf_dev // 2
    for s in range(species):
        for h in range(2):
            first = s * leaf_dev + h * half
            ghosts[h, s] = refitted[first : first + half].astype(jnp.bfloat16)
    equivalent[...] = jnp.dot(
        rounded, up[...], preferred_element_type=jnp.float32
    ).astype(jnp.bfloat16)


def exchange_kernel(n, ghosts, equivalent, before, after, everyone, send, recv, local):
    me = lax.axis_index("seg")
    ahead = [lax.rem(me + p, n) for p in range(n)]
    behind = [lax.rem(me + n - p, n) for p in range(n)]
    greet("seg", ahead[1:])
    own = pltpu.make_async_copy(equivalent, everyone.at[me], local)
    own.start()
    up = remote(ghosts.at[1], before, send.at[0], recv.at[0], "seg", ahead[1])
    down = remote(ghosts.at[0], after, send.at[n], recv.at[n], "seg", behind[1])
    up.start()
    down.start()
    copies = []
    for p in range(1, n):
        copies.append(
            remote(equivalent, everyone.at[me], send.at[p], recv.at[p], "seg", ahead[p])
        )
        copies[-1].start()
    for p in range(1, n):
        slot = everyone.at[behind[p]]
        remote(slot, slot, send.at[p], recv.at[p], "seg", ahead[p]).wait_recv()
    for copy in copies:
        copy.wait_send()
    up.wait()
    down.wait()
    own.wait()


def finish_kernel(
    table, ghosts, before, after, everyone, near_mat, trans, down, out, near_count, far_count
):
    species, slots, width = out.shape
    half = ghosts.shape[2]
    leaf_dev = 2 * half
    me = lax.axis_index("seg")
    n = everyone.shape[0]
    margin = MOVE + REACH
    near_ops = near_mat.shape[0]
    far_ops = trans.shape[0]
    rows = table[pl.ds(pl.multiple_of(me * leaf_dev, 8), slots), :]
    live = rows[:, 0:1] == me
    base = me * leaf_dev - margin
    seen = leaf_dev + 2 * margin
    near_lane = lax.broadcasted_iota(jnp.int32, (slots, seen), 1)
    slot_row = lax.broadcasted_iota(jnp.int32, (slots, seen), 0)
    near_from = rows[:, 1 : 1 + near_count]
    near_kind = rows[:, 1 + near_count : 1 + 2 * near_count]
    far_from = rows[:, 1 + 2 * near_count : 1 + 2 * near_count + far_count]
    near_from = jnp.where(live & (near_from >= 0), near_from - base, -1)
    far_from = jnp.where(live & (far_from >= 0), far_from, -1)
    weights = [((near_lane == slot_row + REACH) & live).astype(jnp.float32)]
    weights += [jnp.zeros((slots, seen), jnp.float32) for _ in range(near_ops)]
    for q in range(near_count):
        hit = near_lane == near_from[:, q : q + 1]
        for o in range(near_ops):
            chosen = hit & (near_kind[:, q : q + 1] == o)
            weights[1 + o] = weights[1 + o] + chosen.astype(jnp.float32)
    weights = jnp.concatenate(weights, axis=0).astype(jnp.bfloat16)
    leaf_total = n * leaf_dev
    far_lane = lax.broadcasted_iota(jnp.int32, (slots, leaf_total), 1)
    picks = jnp.concatenate(
        [(far_lane == far_from[:, o : o + 1]).astype(jnp.float32) for o in range(far_ops)],
        axis=0,
    ).astype(jnp.bfloat16)
    own_term, highs, lows, far_rows = [], [], [], []
    for s in range(species):
        nearby = jnp.concatenate(
            [x.astype(jnp.float32) for x in (before[s], ghosts[0, s], ghosts[1, s], after[s])],
            axis=0,
        ).astype(jnp.bfloat16)
        grouped = jnp.dot(weights, nearby, preferred_element_type=jnp.float32)
        own_term.append(grouped[:slots])
        high, low = split(grouped[slots:])
        highs.append(high)
        lows.append(low)
        source = jnp.concatenate(
            [everyone[e, s * leaf_dev : (s + 1) * leaf_dev, :] for e in range(n)], axis=0
        )
        far_rows.append(
            jnp.dot(picks, source, preferred_element_type=jnp.float32)
        )
    total = jnp.concatenate(own_term, axis=0)
    for o in range(near_ops):
        part = slice(o * slots, (o + 1) * slots)
        stacked = jnp.concatenate(
            [x[part].astype(jnp.float32) for x in highs + lows], axis=0
        ).astype(jnp.bfloat16)
        product = jnp.dot(stacked, near_mat[o], preferred_element_type=jnp.float32)
        total = total + (product[: species * slots] + product[species * slots :])
    expansion = jnp.zeros((species * slots, trans.shape[2]), jnp.float32)
    for o in range(far_ops):
        rows_o = jnp.concatenate(
            [x[o * slots : (o + 1) * slots] for x in far_rows], axis=0
        ).astype(jnp.bfloat16)
        expansion = expansion + jnp.dot(rows_o, trans[o], preferred_element_type=jnp.float32)
    total = total + jnp.dot(
        expansion.astype(jnp.bfloat16), down[...], preferred_element_type=jnp.float32
    )
    for s in range(species):
        out[s] = jnp.where(live, total[s * slots : (s + 1) * slots], 0.0)


def step_kernel(
    n, n_sp, pieces, near_count, far_count,
    coeffs, points_in, owner_in, reaction_in, fit_in, table_in, near_in, up_in, trans_in, down_in,
    out,
    slots, points, owner, reaction, fit, table, near_mat, up, trans, down,
    dense, cheb, fit_high, fit_low, gathered, ghosts, before, after, everyone, weights, picks,
    local, send, recv, sp_send, sp_recv, ex_send, ex_recv,
):
    species, leaf_dev, width = coeffs.shape
    blocks = owner.shape[1]
    count = leaf_dev * blocks
    starts, _ = run_starts()
    me = lax.axis_index("seg")
    me_sp = lax.axis_index("sp")
    half = n // 2
    partner = me + 1 - 2 * lax.rem(me, 2)
    ahead = [lax.rem(me + p, n) for p in range(n)]
    behind = [lax.rem(me + n - p, n) for p in range(n)]
    sp_ahead = [lax.rem(me_sp + p, n_sp) for p in range(n_sp)]
    sp_behind = [lax.rem(me_sp + n_sp - p, n_sp) for p in range(n_sp)]

    moves = [
        (coeffs, slots.at[me]), (points_in, points), (owner_in, owner), (reaction_in, reaction),
        (fit_in, fit), (table_in, table), (near_in, near_mat), (up_in, up), (trans_in, trans),
        (down_in, down),
    ]
    loads = [pltpu.make_async_copy(a, b, local.at[k]) for k, (a, b) in enumerate(moves)]
    for load in loads:
        load.start()

    barrier = pltpu.get_barrier_semaphore()
    for to in ahead[1:]:
        pl.semaphore_signal(barrier, inc=1, device_id={"seg": to}, device_id_type=MESH)
    for to in sp_ahead[1:]:
        pl.semaphore_signal(barrier, inc=1, device_id={"sp": to}, device_id_type=MESH)
    pl.semaphore_wait(barrier, n + n_sp - 2)

    copies = []
    for p in range(1, half):
        copies.append(remote(coeffs, slots.at[me], send.at[p], recv.at[p], "seg", ahead[2 * p]))
        copies[-1].start()
    copies.append(remote(coeffs, slots.at[me], send.at[half], recv.at[half], "seg", partner))
    copies[-1].start()

    loads[1].wait()
    for axis in range(3):
        for m in range(blocks):
            for h in range(leaf_dev // 8):
                x = points[axis, 8 * h : 8 * h + 8, PB * m : PB * m + PB]
                first = 16 * (m * leaf_dev + 8 * h)
                prior, here = jnp.ones_like(x), x
                cheb[axis, pl.ds(first, 8, stride=16), :] = prior
                for d in range(1, ORDER + 1):
                    cheb[axis, pl.ds(first + d, 8, stride=16), :] = here
                    prior, here = here, 2.0 * x * here - prior
                cheb[axis, pl.ds(first + ORDER + 1, 8, stride=16), :] = jnp.zeros_like(x)

    lane = lax.broadcasted_iota(jnp.int32, (8, 128), 1)
    zero = jnp.zeros((8, 128), jnp.float32)
    full = width // 128
    flat = dense.reshape(n * leaf_dev * species * ROWS, 128)

    def expand(slot):
        def chunk(c, carry):
            s = lax.div(c, leaf_dev // 8)
            h = lax.rem(c, leaf_dev // 8)
            part_rows = pl.ds(pl.multiple_of(8 * h, 8), 8)
            tiles = []
            for t in range(full + (width % 128 > 0)):
                if t < full:
                    x = slots[slot, s, part_rows, 128 * t : 128 * t + 128]
                else:
                    x = slots[slot, s, part_rows, 128 * t : width]
                    x = jnp.concatenate(
                        [x, jnp.zeros((8, 128 - width % 128), jnp.float32)], axis=1
                    )
                x_high = x.astype(jnp.bfloat16).astype(jnp.float32)
                tiles.append((x_high, x - x_high))
            base = ((slot * leaf_dev + 8 * h) * species + s) * ROWS
            for g, (i, upper) in enumerate(GROUPS):
                for k in range(8):
                    j = 8 * upper + k
                    if i + j > ORDER:
                        piece = zero
                    else:
                        length = ORDER + 1 - i - j
                        t, shift = divmod(starts[i, j], 128)
                        parts = []
                        for kind in range(2):
                            turn = (128 - shift + 16 * kind) % 128
                            part = tiles[t][kind]
                            if turn:
                                part = pltpu.roll(part, turn, 1)
                            if shift + length > 128:
                                rest = pltpu.roll(tiles[t + 1][kind], turn, 1)
                                part = jnp.where(lane < 128 - shift + 16 * kind, part, rest)
                            parts.append(part)
                        second = jnp.where((lane >= 16) & (lane < 16 + length), parts[1], zero)
                        piece = jnp.where(lane < length, parts[0], second)
                    flat[pl.ds(base + 8 * g + k, 8, stride=species * ROWS), :] = piece
            return carry

        lax.fori_loop(0, species * leaf_dev // 8, chunk, 0)

    loads[0].wait()

    def arrive(p, carry):
        slot = lax.rem(me + n - 2 * p, n)
        other = lax.rem(partner + n - 2 * p, n)

        @pl.when(p > 0)
        def _():
            here = slots.at[slot]
            remote(here, here, send.at[p], recv.at[p], "seg", partner).wait_recv()
            remote(here, here, send.at[half + p], recv.at[half + p], "seg", partner).start()

        expand(slot)
        there = slots.at[other]
        remote(there, there, send.at[half + p], recv.at[half + p], "seg", partner).wait_recv()
        expand(other)

        @pl.when(p == 0)
        def _():
            local_tables()

        return carry

    def local_tables():
        loads[4].wait()
        for k in range(0, fit.shape[0], PB):
            high, low = split(fit[k : k + PB])
            fit_high[k : k + PB] = high
            fit_low[k : k + PB] = low
        loads[5].wait()
        slot_count = out.shape[1]
        rows = table[pl.ds(pl.multiple_of(me * leaf_dev, 8), slot_count), :]
        live = rows[:, 0:1] == me
        margin = MOVE + REACH
        base = me * leaf_dev - margin
        seen = leaf_dev + 2 * margin
        near_lane = lax.broadcasted_iota(jnp.int32, (slot_count, seen), 1)
        slot_row = lax.broadcasted_iota(jnp.int32, (slot_count, seen), 0)
        near_from = rows[:, 1 : 1 + near_count]
        near_kind = rows[:, 1 + near_count : 1 + 2 * near_count]
        far_from = rows[:, 1 + 2 * near_count : 1 + 2 * near_count + far_count]
        near_from = jnp.where(live & (near_from >= 0), near_from - base, -1)
        far_from = jnp.where(live & (far_from >= 0), far_from, -1)
        found = [((near_lane == slot_row + REACH) & live).astype(jnp.float32)]
        found += [jnp.zeros((slot_count, seen), jnp.float32) for _ in range(near_mat.shape[0])]
        for q in range(near_count):
            hit = near_lane == near_from[:, q : q + 1]
            for o in range(near_mat.shape[0]):
                chosen = hit & (near_kind[:, q : q + 1] == o)
                found[1 + o] = found[1 + o] + chosen.astype(jnp.float32)
        weights[...] = jnp.concatenate(found, axis=0).astype(jnp.bfloat16)
        far_lane = lax.broadcasted_iota(jnp.int32, (slot_count, n * leaf_dev), 1)
        picks[...] = jnp.concatenate(
            [(far_lane == far_from[:, o : o + 1]).astype(jnp.float32) for o in range(far_count)],
            axis=0,
        ).astype(jnp.bfloat16)

    lax.fori_loop(0, half, arrive, 0)

    loads[2].wait()

    def block(b):
        leaf = owner[lax.rem(b, leaf_dev), lax.div(b, leaf_dev)]
        lhs = dense[leaf][:, 0:32].astype(jnp.bfloat16)
        here = pl.ds(pl.multiple_of(b * 16, 16), 16)
        tx, ty, tz = cheb[0, here, :], cheb[1, here, :], cheb[2, here, :]
        tz_high = tz.astype(jnp.bfloat16).astype(jnp.float32)
        rhs = jnp.concatenate(
            [
                jnp.concatenate([tz_high, tz - tz_high], axis=1),
                jnp.concatenate([tz_high, jnp.zeros_like(tz)], axis=1),
            ],
            axis=0,
        ).astype(jnp.bfloat16)
        both = jnp.dot(lhs, rhs, preferred_element_type=jnp.float32)
        inner = both[:, :PB] + both[:, PB:]
        for s in range(species):
            total = [None, None]
            for g, (i, upper) in enumerate(GROUPS):
                r = s * ROWS + 8 * g
                term = inner[r : r + 8] * tx[i : i + 1]
                total[upper] = term if total[upper] is None else total[upper] + term
            summed = total[0] * ty[0:8] + total[1] * ty[8:16]
            gathered[me_sp, s, pl.ds(b, 1), :] = jnp.sum(summed, axis=0, keepdims=True)

    step = count // pieces

    def part_of(slot, k):
        return gathered.at[slot, :, step * k : step * (k + 1), :]

    for k in range(pieces):

        def several(c, carry, k=k):
            for u in range(4):
                block(step * k + 4 * c + u)
            return carry

        lax.fori_loop(0, step // 4, several, 0)
        mine = part_of(me_sp, k)
        for p in range(1, n_sp):
            copies.append(
                remote(mine, mine, sp_send.at[k, p], sp_recv.at[k, p], "sp", sp_ahead[p])
            )
            copies[-1].start()

    loads[3].wait()
    rows_total = species * leaf_dev
    refitted = jnp.zeros((rows_total, width), jnp.float32)
    per = step // leaf_dev
    for k in range(pieces):
        for p in range(1, n_sp):
            there = part_of(sp_behind[p], k)
            remote(there, there, sp_send.at[k, p], sp_recv.at[k, p], "sp", sp_ahead[p]).wait_recv()
        by_species = []
        for s in range(species):
            mixing = jnp.zeros((step, PB), jnp.float32)
            for r in range(n_sp * species):
                other = gathered[r // species, r % species, step * k : step * (k + 1), :]
                mixing = mixing + reaction[me_sp * species + s, r] * other
            by_species.append(
                gathered[me_sp, s, step * k : step * (k + 1), :] + jnp.tanh(mixing)
            )
        reacted = jnp.concatenate(
            [
                jnp.concatenate(
                    [x[m * leaf_dev : (m + 1) * leaf_dev] for x in by_species], axis=0
                )
                for m in range(per)
            ],
            axis=1,
        )
        high, low = split(reacted)
        nodes = slice(k * per * PB, (k + 1) * per * PB)
        main = jnp.dot(
            jnp.concatenate([high, low], axis=0), fit_high[nodes],
            preferred_element_type=jnp.float32,
        )
        rest = jnp.dot(high, fit_low[nodes], preferred_element_type=jnp.float32)
        refitted = refitted + (main[:rows_total] + (main[rows_total:] + rest))
    rounded = refitted.astype(jnp.bfloat16)
    half_leaf = leaf_dev // 2
    for s in range(species):
        for h in range(2):
            first = s * leaf_dev + h * half_leaf
            ghosts[h, s] = refitted[first : first + half_leaf].astype(jnp.bfloat16)
    rise = remote(ghosts.at[1], before, ex_send.at[0], ex_recv.at[0], "seg", ahead[1])
    fall = remote(ghosts.at[0], after, ex_send.at[n], ex_recv.at[n], "seg", behind[1])
    loads[7].wait()
    everyone[me] = jnp.dot(
        rounded, up[...], preferred_element_type=jnp.float32
    ).astype(jnp.bfloat16)
    for p in range(1, n):
        mine = everyone.at[me]
        copies.append(remote(mine, mine, ex_send.at[p], ex_recv.at[p], "seg", ahead[p]))
        copies[-1].start()
    rise.start()
    fall.start()

    near_ops, far_ops = near_mat.shape[0], trans.shape[0]
    slot_count = out.shape[1]
    loads[6].wait()
    loads[8].wait()
    loads[9].wait()
    rise.wait()
    fall.wait()
    own_term, highs, lows = [], [], []
    for s in range(species):
        nearby = jnp.concatenate(
            [x.astype(jnp.float32) for x in (before[s], ghosts[0, s], ghosts[1, s], after[s])],
            axis=0,
        ).astype(jnp.bfloat16)
        grouped = jnp.dot(weights[...], nearby, preferred_element_type=jnp.float32)
        own_term.append(grouped[:slot_count])
        high, low = split(grouped[slot_count:])
        highs.append(high)
        lows.append(low)
    total = jnp.concatenate(own_term, axis=0)
    for o in range(near_ops):
        part = slice(o * slot_count, (o + 1) * slot_count)
        stacked = jnp.concatenate(
            [x[part].astype(jnp.float32) for x in highs + lows], axis=0
        ).astype(jnp.bfloat16)
        product = jnp.dot(stacked, near_mat[o], preferred_element_type=jnp.float32)
        total = total + (product[: species * slot_count] + product[species * slot_count :])
    for p in range(1, n):
        there = everyone.at[behind[p]]
        remote(there, there, ex_send.at[p], ex_recv.at[p], "seg", ahead[p]).wait_recv()
    far_rows = []
    for s in range(species):
        source = jnp.concatenate(
            [everyone[e, s * leaf_dev : (s + 1) * leaf_dev, :] for e in range(n)], axis=0
        )
        far_rows.append(jnp.dot(picks[...], source, preferred_element_type=jnp.float32))
    expansion = jnp.zeros((species * slot_count, trans.shape[2]), jnp.float32)
    for o in range(far_ops):
        rows_o = jnp.concatenate(
            [x[o * slot_count : (o + 1) * slot_count] for x in far_rows], axis=0
        ).astype(jnp.bfloat16)
        expansion = expansion + jnp.dot(rows_o, trans[o], preferred_element_type=jnp.float32)
    total = total + jnp.dot(
        expansion.astype(jnp.bfloat16), down[...], preferred_element_type=jnp.float32
    )
    live = table[pl.ds(pl.multiple_of(me * leaf_dev, 8), slot_count), 0:1] == me
    for s in range(species):
        out[s] = jnp.where(live, total[s * slot_count : (s + 1) * slot_count], 0.0)
    for copy in copies:
        copy.wait_send()
    for p in range(1, half):
        there = slots.at[behind[2 * p]]
        remote(there, there, send.at[half + p], recv.at[half + p], "seg", partner).wait_send()


def whole_step(
    coeffs, points, owner_leaf, reaction, fit_matrix, table, near_mat, up_mat, trans_mat,
    down_mat, near_count, far_count,
):
    species, leaf_dev, width = coeffs.shape
    n, n_sp = lax.axis_size("seg"), lax.axis_size("sp")
    blocks = owner_leaf.shape[1]
    count = leaf_dev * blocks
    slots = leaf_dev + 2 * MOVE
    seen = leaf_dev + 2 * (MOVE + REACH)
    half = leaf_dev // 2
    pieces = 3
    f32, bf16, i32 = jnp.float32, jnp.bfloat16, jnp.int32
    dma = pltpu.SemaphoreType.DMA
    return pl.pallas_call(
        functools.partial(step_kernel, n, n_sp, pieces, near_count, far_count),
        out_shape=jax.ShapeDtypeStruct((species, slots, width), f32),
        in_specs=[ANY] * 10,
        out_specs=VMEM,
        scratch_shapes=[
            pltpu.VMEM((n,) + coeffs.shape, f32),
            pltpu.VMEM(points.shape, f32),
            pltpu.SMEM(owner_leaf.shape, i32),
            pltpu.SMEM(reaction.shape, f32),
            pltpu.VMEM(fit_matrix.shape, f32),
            pltpu.VMEM(table.shape, i32),
            pltpu.VMEM(near_mat.shape, bf16),
            pltpu.VMEM(up_mat.shape, bf16),
            pltpu.VMEM(trans_mat.shape, bf16),
            pltpu.VMEM(down_mat.shape, bf16),
            pltpu.VMEM((n * leaf_dev, species * ROWS, 128), f32),
            pltpu.VMEM((3, 16 * count, PB), f32),
            pltpu.VMEM(fit_matrix.shape, bf16),
            pltpu.VMEM(fit_matrix.shape, bf16),
            pltpu.VMEM((n_sp, species, count, PB), f32),
            pltpu.VMEM((2, species, half, width), bf16),
            pltpu.VMEM((species, half, width), bf16),
            pltpu.VMEM((species, half, width), bf16),
            pltpu.VMEM((n, species * leaf_dev, up_mat.shape[1]), bf16),
            pltpu.VMEM(((1 + near_mat.shape[0]) * slots, seen), bf16),
            pltpu.VMEM((far_count * slots, n * leaf_dev), bf16),
            dma((10,)), dma((n,)), dma((n,)), dma((pieces, n_sp)), dma((pieces, n_sp)),
            dma((n + 1,)), dma((n + 1,)),
        ],
        compiler_params=pltpu.CompilerParams(
            collective_id=3, has_side_effects=True, vmem_limit_bytes=LIMIT
        ),
        name="step",
    )(
        coeffs, points, owner_leaf, reaction, fit_matrix, table, near_mat, up_mat, trans_mat,
        down_mat,
    )


def shards(
    coeffs, points, owner_leaf, reaction, fit_matrix, new_seg, near_src, near_op,
    near_mat, up_mat, far_src, trans_mat, down_mat,
):
    species, leaf_dev, width = coeffs.shape
    n = lax.axis_size("seg")
    blocks = owner_leaf.shape[1]
    count = leaf_dev * blocks
    padded_width = -(-width // 128) * 128
    slots = leaf_dev + 2 * MOVE
    table = jnp.concatenate([new_seg[:, None], near_src, near_op, far_src], axis=1)
    table = jnp.pad(table, ((MOVE, MOVE), (0, 0)), constant_values=-1)
    if n * leaf_dev * species * ROWS * 512 <= LIMIT // 2:
        return whole_step(
            coeffs, points, owner_leaf, reaction, fit_matrix, table, near_mat, up_mat,
            trans_mat, down_mat, near_src.shape[1], far_src.shape[1],
        )
    mine = jnp.transpose(coeffs, (1, 0, 2))
    everyone = pair_gather(mine, "seg", 0).reshape(n * leaf_dev, species, width)
    values = pl.pallas_call(
        evaluate_kernel,
        out_shape=jax.ShapeDtypeStruct((species, count, PB), jnp.float32),
        in_specs=[SMEM, VMEM, VMEM],
        out_specs=VMEM,
        scratch_shapes=[
            pltpu.VMEM((8, padded_width), jnp.float32),
            pltpu.VMEM((count * species * ROWS, 128), jnp.float32),
            pltpu.VMEM((3, 16 * count, PB), jnp.float32),
        ],
        compiler_params=pltpu.CompilerParams(vmem_limit_bytes=LIMIT),
        name="evaluate",
    )(owner_leaf, everyone, points)
    gathered = pair_gather(values, "sp", 1)
    half = leaf_dev // 2
    ghosts, equivalent = pl.pallas_call(
        refit_kernel,
        out_shape=(
            jax.ShapeDtypeStruct((2, species, half, width), jnp.bfloat16),
            jax.ShapeDtypeStruct((species * leaf_dev, up_mat.shape[1]), jnp.bfloat16),
        ),
        in_specs=[SMEM, VMEM, VMEM, VMEM, VMEM],
        out_specs=(VMEM, VMEM),
        scratch_shapes=[pltpu.VMEM((species * leaf_dev, blocks * PB), jnp.float32)],
        compiler_params=pltpu.CompilerParams(vmem_limit_bytes=LIMIT),
        name="refit",
    )(reaction, values, gathered, fit_matrix, up_mat)
    before, after, all_equivalent = pl.pallas_call(
        functools.partial(exchange_kernel, n),
        out_shape=(
            jax.ShapeDtypeStruct((species, half, width), jnp.bfloat16),
            jax.ShapeDtypeStruct((species, half, width), jnp.bfloat16),
            jax.ShapeDtypeStruct((n,) + equivalent.shape, jnp.bfloat16),
        ),
        in_specs=[ANY, ANY],
        out_specs=(ANY, ANY, ANY),
        scratch_shapes=[
            pltpu.SemaphoreType.DMA((n + 1,)),
            pltpu.SemaphoreType.DMA((n + 1,)),
            pltpu.SemaphoreType.DMA,
        ],
        compiler_params=pltpu.CompilerParams(collective_id=2, has_side_effects=True),
        name="exchange",
    )(ghosts, equivalent)
    return pl.pallas_call(
        functools.partial(
            finish_kernel, near_count=near_src.shape[1], far_count=far_src.shape[1]
        ),
        out_shape=jax.ShapeDtypeStruct((species, slots, width), jnp.float32),
        in_specs=[VMEM] * 8,
        out_specs=VMEM,
        compiler_params=pltpu.CompilerParams(vmem_limit_bytes=LIMIT),
        name="finish",
    )(table, ghosts, before, after, all_equivalent, near_mat, trans_mat, down_mat)


def solution(mesh):
    placed = (P("sp", "seg", None), P(None, "seg", None), P("seg", None)) + (P(),) * 10
    return jax.shard_map(
        shards, mesh=mesh, in_specs=placed, out_specs=P("sp", "seg", None), check_vma=False
    )
```

```python
import functools

import jax
import jax.numpy as jnp
import numpy as np
from jax import lax
from jax.experimental import pallas as pl
from jax.experimental.pallas import tpu as pltpu
from jax.sharding import PartitionSpec as P

ORDER = 14
PB = 128
MOVE = 4
REACH = 4
MESH = pl.DeviceIdType.MESH
VMEM = pl.BlockSpec(memory_space=pltpu.VMEM)
SMEM = pl.BlockSpec(memory_space=pltpu.SMEM)
ANY = pl.BlockSpec(memory_space=pl.ANY)
LIMIT = 60 * 1024 * 1024


def run_starts():
    starts, counter = {}, 0
    for i in range(ORDER + 1):
        for j in range(ORDER + 1 - i):
            starts[i, j] = counter
            counter += ORDER + 1 - i - j
    return starts, counter


GROUPS = [(i, 0) for i in range(ORDER + 1)] + [(i, 1) for i in range(ORDER + 1 - 8)]
ROWS = 8 * len(GROUPS)


def remote(src, dst, send, recv, axis, to):
    return pltpu.make_async_remote_copy(
        src_ref=src, dst_ref=dst, send_sem=send, recv_sem=recv,
        device_id={axis: to}, device_id_type=MESH,
    )


def greet(axis, others):
    barrier = pltpu.get_barrier_semaphore()
    for to in others:
        pl.semaphore_signal(barrier, inc=1, device_id={axis: to}, device_id_type=MESH)
    pl.semaphore_wait(barrier, len(others))


def pair_gather_kernel(axis, n, src, out, send, recv, local):
    me = lax.axis_index(axis)
    half = n // 2
    partner = me + 1 - 2 * lax.rem(me, 2)
    ahead = [lax.rem(me + 2 * p, n) for p in range(half)]
    behind = [lax.rem(me + n - 2 * p, n) for p in range(half)]
    partner_behind = [lax.rem(partner + n - 2 * p, n) for p in range(half)]
    greet(axis, ahead[1:] + [partner])
    own = pltpu.make_async_copy(src, out.at[me], local)
    own.start()
    copies = []
    for p in range(1, half):
        copies.append(remote(src, out.at[me], send.at[p], recv.at[p], axis, ahead[p]))
        copies[-1].start()
    copies.append(remote(src, out.at[me], send.at[half], recv.at[half], axis, partner))
    copies[-1].start()
    for p in range(1, half):
        slot = out.at[behind[p]]
        remote(slot, slot, send.at[p], recv.at[p], axis, partner).wait_recv()
        copies.append(remote(slot, slot, send.at[half + p], recv.at[half + p], axis, partner))
        copies[-1].start()
    for p in range(half):
        slot = out.at[partner_behind[p]]
        remote(slot, slot, send.at[half + p], recv.at[half + p], axis, partner).wait_recv()
    for copy in copies:
        copy.wait_send()
    own.wait()


def pair_gather(value, axis, collective_id):
    n = lax.axis_size(axis)
    return pl.pallas_call(
        functools.partial(pair_gather_kernel, axis, n),
        out_shape=jax.ShapeDtypeStruct((n,) + value.shape, value.dtype),
        in_specs=[ANY],
        out_specs=ANY,
        scratch_shapes=[
            pltpu.SemaphoreType.DMA((n,)),
            pltpu.SemaphoreType.DMA((n,)),
            pltpu.SemaphoreType.DMA,
        ],
        compiler_params=pltpu.CompilerParams(
            collective_id=collective_id, has_side_effects=True
        ),
        name="gather_" + axis,
    )(value)


def evaluate_kernel(owner, coef, points, values, rows, dense, cheb):
    leaf_dev, blocks = owner.shape
    species = values.shape[0]
    width = coef.shape[2]
    starts, _ = run_starts()
    chunk = 8 // species
    for axis in range(3):
        for m in range(blocks):
            for h in range(leaf_dev // 8):
                x = points[axis, 8 * h : 8 * h + 8, PB * m : PB * m + PB]
                first = 16 * (m * leaf_dev + 8 * h)
                below, here = jnp.ones_like(x), x
                cheb[axis, pl.ds(first, 8, stride=16), :] = below
                for d in range(1, ORDER + 1):
                    cheb[axis, pl.ds(first + d, 8, stride=16), :] = here
                    below, here = here, 2.0 * x * here - below
                cheb[axis, pl.ds(first + ORDER + 1, 8, stride=16), :] = jnp.zeros_like(x)
    lane = lax.broadcasted_iota(jnp.int32, (8, 128), 1)

    def expand(c, carry):
        for k in range(chunk):
            b = c * chunk + k
            leaf = owner[lax.rem(b, leaf_dev), lax.div(b, leaf_dev)]
            rows[species * k : species * (k + 1), :width] = coef[leaf]
        tiles = []
        for t in range(rows.shape[1] // 128):
            x = rows[:, 128 * t : 128 * t + 128]
            x_high = x.astype(jnp.bfloat16).astype(jnp.float32)
            tiles.append((x_high, x - x_high))
        zero = jnp.zeros((8, 128), jnp.float32)
        for g, (i, upper) in enumerate(GROUPS):
            for k in range(8):
                j = 8 * upper + k
                if i + j > ORDER:
                    piece = zero
                else:
                    length = ORDER + 1 - i - j
                    t, shift = divmod(starts[i, j], 128)
                    parts = []
                    for kind in range(2):
                        turn = (128 - shift + 16 * kind) % 128
                        part = tiles[t][kind]
                        if turn:
                            part = pltpu.roll(part, turn, 1)
                        if shift + length > 128:
                            rest = pltpu.roll(tiles[t + 1][kind], turn, 1)
                            part = jnp.where(lane < 128 - shift + 16 * kind, part, rest)
                        parts.append(part)
                    second = jnp.where((lane >= 16) & (lane < 16 + length), parts[1], zero)
                    piece = jnp.where(lane < length, parts[0], second)
                dense[pl.ds(c * (8 * ROWS) + 8 * g + k, 8, stride=ROWS), :] = piece
        return carry

    lax.fori_loop(0, leaf_dev * blocks // chunk, expand, 0)

    def block(b):
        lhs = dense[pl.ds(b * (species * ROWS), species * ROWS), 0:32].astype(jnp.bfloat16)
        tx = cheb[0, pl.ds(b * 16, 16), :]
        ty = cheb[1, pl.ds(b * 16, 16), :]
        tz = cheb[2, pl.ds(b * 16, 16), :]
        high = tz.astype(jnp.bfloat16)
        tz_high = high.astype(jnp.float32)
        rhs = jnp.concatenate(
            [
                jnp.concatenate([tz_high, tz - tz_high], axis=1),
                jnp.concatenate([tz_high, jnp.zeros_like(tz)], axis=1),
            ],
            axis=0,
        ).astype(jnp.bfloat16)
        both = jnp.dot(lhs, rhs, preferred_element_type=jnp.float32)
        inner = both[:, :PB] + both[:, PB:]
        for s in range(species):
            total = [None, None]
            for g, (i, upper) in enumerate(GROUPS):
                r = s * ROWS + 8 * g
                term = inner[r : r + 8] * tx[i : i + 1]
                total[upper] = term if total[upper] is None else total[upper] + term
            summed = total[0] * ty[0:8] + total[1] * ty[8:16]
            values[s, pl.ds(b, 1), :] = jnp.sum(summed, axis=0, keepdims=True)

    def pair(c, carry):
        for k in range(4):
            block(4 * c + k)
        return carry

    lax.fori_loop(0, leaf_dev * blocks // 4, pair, 0)


def split(x):
    high = x.astype(jnp.bfloat16)
    return high, (x - high.astype(jnp.float32)).astype(jnp.bfloat16)


def refit_kernel(reaction, own, gathered, fit, up, ghosts, equivalent, reacted):
    species, block_count, _ = own.shape
    leaf_dev = equivalent.shape[0] // species
    blocks = block_count // leaf_dev
    total_species = reaction.shape[1]
    start = lax.axis_index("sp") * species
    for s in range(species):
        mixing = jnp.zeros((block_count, PB), jnp.float32)
        for r in range(total_species):
            other = gathered[r // species, r % species].astype(jnp.float32)
            mixing = mixing + reaction[start + s, r] * other
        result = own[s] + jnp.tanh(mixing)
        for m in range(blocks):
            reacted[s * leaf_dev : (s + 1) * leaf_dev, m * PB : (m + 1) * PB] = result[
                m * leaf_dev : (m + 1) * leaf_dev
            ]
    high, low = split(reacted[...])
    fit_high, fit_low = split(fit[...])
    main = jnp.dot(
        jnp.concatenate([high, low], axis=0), fit_high, preferred_element_type=jnp.float32
    )
    rest = jnp.dot(high, fit_low, preferred_element_type=jnp.float32)
    count = species * leaf_dev
    refitted = main[:count] + (main[count:] + rest)
    rounded = refitted.astype(jnp.bfloat16)
    half = leaf_dev // 2
    for s in range(species):
        for h in range(2):
            first = s * leaf_dev + h * half
            ghosts[h, s] = refitted[first : first + half].astype(jnp.bfloat16)
    equivalent[...] = jnp.dot(
        rounded, up[...], preferred_element_type=jnp.float32
    ).astype(jnp.bfloat16)


def exchange_kernel(n, ghosts, equivalent, before, after, everyone, send, recv, local):
    me = lax.axis_index("seg")
    ahead = [lax.rem(me + p, n) for p in range(n)]
    behind = [lax.rem(me + n - p, n) for p in range(n)]
    greet("seg", ahead[1:])
    own = pltpu.make_async_copy(equivalent, everyone.at[me], local)
    own.start()
    up = remote(ghosts.at[1], before, send.at[0], recv.at[0], "seg", ahead[1])
    down = remote(ghosts.at[0], after, send.at[n], recv.at[n], "seg", behind[1])
    up.start()
    down.start()
    copies = []
    for p in range(1, n):
        copies.append(
            remote(equivalent, everyone.at[me], send.at[p], recv.at[p], "seg", ahead[p])
        )
        copies[-1].start()
    for p in range(1, n):
        slot = everyone.at[behind[p]]
        remote(slot, slot, send.at[p], recv.at[p], "seg", ahead[p]).wait_recv()
    for copy in copies:
        copy.wait_send()
    up.wait()
    down.wait()
    own.wait()


def finish_kernel(
    table, ghosts, before, after, everyone, near_mat, trans, down, out, near_count, far_count
):
    species, slots, width = out.shape
    half = ghosts.shape[2]
    leaf_dev = 2 * half
    me = lax.axis_index("seg")
    n = everyone.shape[0]
    margin = MOVE + REACH
    near_ops = near_mat.shape[0]
    far_ops = trans.shape[0]
    rows = table[pl.ds(pl.multiple_of(me * leaf_dev, 8), slots), :]
    live = rows[:, 0:1] == me
    base = me * leaf_dev - margin
    seen = leaf_dev + 2 * margin
    near_lane = lax.broadcasted_iota(jnp.int32, (slots, seen), 1)
    slot_row = lax.broadcasted_iota(jnp.int32, (slots, seen), 0)
    near_from = rows[:, 1 : 1 + near_count]
    near_kind = rows[:, 1 + near_count : 1 + 2 * near_count]
    far_from = rows[:, 1 + 2 * near_count : 1 + 2 * near_count + far_count]
    near_from = jnp.where(live & (near_from >= 0), near_from - base, -1)
    far_from = jnp.where(live & (far_from >= 0), far_from, -1)
    weights = [((near_lane == slot_row + REACH) & live).astype(jnp.float32)]
    weights += [jnp.zeros((slots, seen), jnp.float32) for _ in range(near_ops)]
    for q in range(near_count):
        hit = near_lane == near_from[:, q : q + 1]
        for o in range(near_ops):
            chosen = hit & (near_kind[:, q : q + 1] == o)
            weights[1 + o] = weights[1 + o] + chosen.astype(jnp.float32)
    weights = jnp.concatenate(weights, axis=0).astype(jnp.bfloat16)
    leaf_total = n * leaf_dev
    far_lane = lax.broadcasted_iota(jnp.int32, (slots, leaf_total), 1)
    picks = jnp.concatenate(
        [(far_lane == far_from[:, o : o + 1]).astype(jnp.float32) for o in range(far_ops)],
        axis=0,
    ).astype(jnp.bfloat16)
    own_term, highs, lows, far_rows = [], [], [], []
    for s in range(species):
        nearby = jnp.concatenate(
            [x.astype(jnp.float32) for x in (before[s], ghosts[0, s], ghosts[1, s], after[s])],
            axis=0,
        ).astype(jnp.bfloat16)
        grouped = jnp.dot(weights, nearby, preferred_element_type=jnp.float32)
        own_term.append(grouped[:slots])
        high, low = split(grouped[slots:])
        highs.append(high)
        lows.append(low)
        source = jnp.concatenate(
            [everyone[e, s * leaf_dev : (s + 1) * leaf_dev, :] for e in range(n)], axis=0
        )
        far_rows.append(
            jnp.dot(picks, source, preferred_element_type=jnp.float32)
        )
    total = jnp.concatenate(own_term, axis=0)
    for o in range(near_ops):
        part = slice(o * slots, (o + 1) * slots)
        stacked = jnp.concatenate(
            [x[part].astype(jnp.float32) for x in highs + lows], axis=0
        ).astype(jnp.bfloat16)
        product = jnp.dot(stacked, near_mat[o], preferred_element_type=jnp.float32)
        total = total + (product[: species * slots] + product[species * slots :])
    expansion = jnp.zeros((species * slots, trans.shape[2]), jnp.float32)
    for o in range(far_ops):
        rows_o = jnp.concatenate(
            [x[o * slots : (o + 1) * slots] for x in far_rows], axis=0
        ).astype(jnp.bfloat16)
        expansion = expansion + jnp.dot(rows_o, trans[o], preferred_element_type=jnp.float32)
    total = total + jnp.dot(
        expansion.astype(jnp.bfloat16), down[...], preferred_element_type=jnp.float32
    )
    for s in range(species):
        out[s] = jnp.where(live, total[s * slots : (s + 1) * slots], 0.0)


def last_dims(x, y):
    return lax.dot_general(
        x, y, (((1,), (1,)), ((), ())), preferred_element_type=jnp.float32
    )


def step_kernel(
    n, n_sp, pieces, near_count, far_count,
    coeffs, points_in, owner_in, reaction_in, fit_in, table_in, near_in, up_in, trans_in, down_in,
    out,
    slots, points, owner, reaction, fit, table, near_mat, up, trans, down,
    dense, cheb, fit_high, fit_low, gathered, ghosts, before, after, everyone, weights, picks,
    local, send, recv, sp_send, sp_recv, ex_send, ex_recv,
):
    species, leaf_dev, width = coeffs.shape
    blocks = owner.shape[0]
    count = leaf_dev * blocks
    starts, _ = run_starts()
    me = lax.axis_index("seg")
    me_sp = lax.axis_index("sp")
    half = n // 2
    partner = me + 1 - 2 * lax.rem(me, 2)
    ahead = [lax.rem(me + p, n) for p in range(n)]
    behind = [lax.rem(me + n - p, n) for p in range(n)]
    sp_ahead = [lax.rem(me_sp + p, n_sp) for p in range(n_sp)]
    sp_behind = [lax.rem(me_sp + n_sp - p, n_sp) for p in range(n_sp)]

    moves = [
        (coeffs, slots.at[me]), (points_in, points), (owner_in, owner), (reaction_in, reaction),
        (fit_in, fit), (table_in, table), (near_in, near_mat), (up_in, up), (trans_in, trans),
        (down_in, down),
    ]
    loads = [pltpu.make_async_copy(a, b, local.at[k]) for k, (a, b) in enumerate(moves)]
    for load in loads:
        load.start()

    barrier = pltpu.get_barrier_semaphore()
    for to in ahead[1:]:
        pl.semaphore_signal(barrier, inc=1, device_id={"seg": to}, device_id_type=MESH)
    for to in sp_ahead[1:]:
        pl.semaphore_signal(barrier, inc=1, device_id={"sp": to}, device_id_type=MESH)
    pl.semaphore_wait(barrier, n + n_sp - 2)

    copies = []
    for p in range(1, half):
        copies.append(remote(coeffs, slots.at[me], send.at[p], recv.at[p], "seg", ahead[2 * p]))
        copies[-1].start()
    copies.append(remote(coeffs, slots.at[me], send.at[half], recv.at[half], "seg", partner))
    copies[-1].start()

    loads[1].wait()
    for axis in range(3):
        for m in range(blocks):
            for h in range(leaf_dev // 8):
                x = points[axis, 8 * h : 8 * h + 8, PB * m : PB * m + PB]
                first = 16 * (m * leaf_dev + 8 * h)
                prior, here = jnp.ones_like(x), x
                cheb[axis, pl.ds(first, 8, stride=16), :] = prior
                for d in range(1, ORDER + 1):
                    cheb[axis, pl.ds(first + d, 8, stride=16), :] = here
                    prior, here = here, 2.0 * x * here - prior
                cheb[axis, pl.ds(first + ORDER + 1, 8, stride=16), :] = jnp.zeros_like(x)

    lane = lax.broadcasted_iota(jnp.int32, (8, 128), 1)
    zero = jnp.zeros((8, 128), jnp.float32)
    full = width // 128
    flat = dense.reshape(n * leaf_dev * species * ROWS, 128)

    def expand(slot):
        def chunk(c, carry):
            s = lax.div(c, leaf_dev // 8)
            h = lax.rem(c, leaf_dev // 8)
            part_rows = pl.ds(pl.multiple_of(8 * h, 8), 8)
            tiles = []
            for t in range(full + (width % 128 > 0)):
                if t < full:
                    x = slots[slot, s, part_rows, 128 * t : 128 * t + 128]
                else:
                    x = slots[slot, s, part_rows, 128 * t : width]
                    x = jnp.concatenate(
                        [x, jnp.zeros((8, 128 - width % 128), jnp.float32)], axis=1
                    )
                x_high = x.astype(jnp.bfloat16).astype(jnp.float32)
                tiles.append((x_high, x - x_high))
            base = ((slot * leaf_dev + 8 * h) * species + s) * ROWS
            for g, (i, upper) in enumerate(GROUPS):
                for k in range(8):
                    j = 8 * upper + k
                    if i + j <= ORDER:
                        length = ORDER + 1 - i - j
                        t, shift = divmod(starts[i, j], 128)
                        parts = []
                        for kind in range(2):
                            turn = (128 - shift + 16 * kind) % 128
                            part = tiles[t][kind]
                            if turn:
                                part = pltpu.roll(part, turn, 1)
                            if shift + length > 128:
                                rest = pltpu.roll(tiles[t + 1][kind], turn, 1)
                                part = jnp.where(lane < 128 - shift + 16 * kind, part, rest)
                            parts.append(part)
                        second = jnp.where((lane >= 16) & (lane < 16 + length), parts[1], zero)
                        piece = jnp.where(lane < length, parts[0], second)
                        flat[pl.ds(base + 8 * g + k, 8, stride=species * ROWS), :] = piece
            return carry

        lax.fori_loop(0, species * leaf_dev // 8, chunk, 0)

    partial = [g for g, (i, upper) in enumerate(GROUPS) if i + 8 * upper + 7 > ORDER]

    def clear(leaf, carry):
        for s in range(species):
            for g in partial:
                dense[leaf, s * ROWS + 8 * g : s * ROWS + 8 * g + 8, :] = zero
        return carry

    lax.fori_loop(0, n * leaf_dev, clear, 0)
    loads[0].wait()

    def arrive(p, carry):
        slot = lax.rem(me + n - 2 * p, n)
        other = lax.rem(partner + n - 2 * p, n)

        @pl.when(p > 0)
        def _():
            here = slots.at[slot]
            remote(here, here, send.at[p], recv.at[p], "seg", partner).wait_recv()
            remote(here, here, send.at[half + p], recv.at[half + p], "seg", partner).start()

        expand(slot)
        there = slots.at[other]
        remote(there, there, send.at[half + p], recv.at[half + p], "seg", partner).wait_recv()
        expand(other)

        @pl.when(p == 0)
        def _():
            local_tables()

        return carry

    def local_tables():
        loads[4].wait()
        for k in range(0, fit.shape[0], PB):
            high, low = split(fit[k : min(k + PB, width)])
            fit_high[k : min(k + PB, width)] = high
            fit_low[k : min(k + PB, width)] = low
        loads[5].wait()
        slot_count = out.shape[1]
        rows = table[pl.ds(pl.multiple_of(me * leaf_dev, 8), slot_count), :]
        live = rows[:, 0:1] == me
        margin = MOVE + REACH
        base = me * leaf_dev - margin
        seen = leaf_dev + 2 * margin
        near_lane = lax.broadcasted_iota(jnp.int32, (slot_count, seen), 1)
        slot_row = lax.broadcasted_iota(jnp.int32, (slot_count, seen), 0)
        near_from = rows[:, 1 : 1 + near_count]
        near_kind = rows[:, 1 + near_count : 1 + 2 * near_count]
        far_from = rows[:, 1 + 2 * near_count : 1 + 2 * near_count + far_count]
        near_from = jnp.where(live & (near_from >= 0), near_from - base, -1)
        far_from = jnp.where(live & (far_from >= 0), far_from, -1)
        found = [((near_lane == slot_row + REACH) & live).astype(jnp.float32)]
        found += [jnp.zeros((slot_count, seen), jnp.float32) for _ in range(near_mat.shape[0])]
        for q in range(near_count):
            hit = near_lane == near_from[:, q : q + 1]
            for o in range(near_mat.shape[0]):
                chosen = hit & (near_kind[:, q : q + 1] == o)
                found[1 + o] = found[1 + o] + chosen.astype(jnp.float32)
        weights[...] = jnp.concatenate(found, axis=0).astype(jnp.bfloat16)
        far_lane = lax.broadcasted_iota(jnp.int32, (slot_count, n * leaf_dev), 1)
        picks[...] = jnp.concatenate(
            [(far_lane == far_from[:, o : o + 1]).astype(jnp.float32) for o in range(far_count)],
            axis=0,
        ).astype(jnp.bfloat16)

    lax.fori_loop(0, half, arrive, 0)

    loads[2].wait()

    def block(b):
        leaf = owner[lax.div(b, leaf_dev), lax.rem(b, leaf_dev)]
        lhs = dense[leaf][:, 0:32].astype(jnp.bfloat16)
        here = pl.ds(pl.multiple_of(b * 16, 16), 16)
        tx, ty, tz = cheb[0, here, :], cheb[1, here, :], cheb[2, here, :]
        tz_high = tz.astype(jnp.bfloat16).astype(jnp.float32)
        rhs = jnp.concatenate(
            [
                jnp.concatenate([tz_high, tz - tz_high], axis=1),
                jnp.concatenate([tz_high, jnp.zeros_like(tz)], axis=1),
            ],
            axis=0,
        ).astype(jnp.bfloat16)
        both = jnp.dot(lhs, rhs, preferred_element_type=jnp.float32)
        inner = both[:, :PB] + both[:, PB:]
        for s in range(species):
            total = [None, None]
            for g, (i, upper) in enumerate(GROUPS):
                r = s * ROWS + 8 * g
                term = inner[r : r + 8] * tx[i : i + 1]
                total[upper] = term if total[upper] is None else total[upper] + term
            summed = total[0] * ty[0:8] + total[1] * ty[8:16]
            gathered[me_sp, s, pl.ds(b, 1), :] = jnp.sum(summed, axis=0, keepdims=True)

    step = count // pieces

    def part_of(slot, k):
        return gathered.at[slot, :, step * k : step * (k + 1), :]

    for k in range(pieces):

        def several(c, carry, k=k):
            for u in range(4):
                block(step * k + 4 * c + u)
            return carry

        lax.fori_loop(0, step // 4, several, 0)
        mine = part_of(me_sp, k)
        for p in range(1, n_sp):
            copies.append(
                remote(mine, mine, sp_send.at[k, p], sp_recv.at[k, p], "sp", sp_ahead[p])
            )
            copies[-1].start()

    loads[3].wait()
    rows_total = species * leaf_dev
    refitted = jnp.zeros((rows_total, width), jnp.float32)
    per = step // leaf_dev
    for k in range(pieces):
        for p in range(1, n_sp):
            there = part_of(sp_behind[p], k)
            remote(there, there, sp_send.at[k, p], sp_recv.at[k, p], "sp", sp_ahead[p]).wait_recv()
        by_species = []
        for s in range(species):
            mixing = jnp.zeros((step, PB), jnp.float32)
            for r in range(n_sp * species):
                other = gathered[r // species, r % species, step * k : step * (k + 1), :]
                mixing = mixing + reaction[me_sp * species + s, r] * other
            by_species.append(
                gathered[me_sp, s, step * k : step * (k + 1), :] + jnp.tanh(mixing)
            )
        reacted = jnp.concatenate(
            [
                jnp.concatenate(
                    [x[m * leaf_dev : (m + 1) * leaf_dev] for x in by_species], axis=0
                )
                for m in range(per)
            ],
            axis=1,
        )
        high, low = split(reacted)
        nodes = slice(k * per * PB, (k + 1) * per * PB)
        main = last_dims(jnp.concatenate([high, low], axis=0), fit_high[:, nodes])
        rest = last_dims(high, fit_low[:, nodes])
        refitted = refitted + (main[:rows_total] + (main[rows_total:] + rest))
    rounded = refitted.astype(jnp.bfloat16)
    half_leaf = leaf_dev // 2
    for s in range(species):
        for h in range(2):
            first = s * leaf_dev + h * half_leaf
            ghosts[h, s] = refitted[first : first + half_leaf].astype(jnp.bfloat16)
    rise = remote(ghosts.at[1], before, ex_send.at[0], ex_recv.at[0], "seg", ahead[1])
    fall = remote(ghosts.at[0], after, ex_send.at[n], ex_recv.at[n], "seg", behind[1])
    loads[7].wait()
    everyone[me] = last_dims(rounded, up[...]).astype(jnp.bfloat16)
    for p in range(1, n):
        mine = everyone.at[me]
        copies.append(remote(mine, mine, ex_send.at[p], ex_recv.at[p], "seg", ahead[p]))
        copies[-1].start()
    rise.start()
    fall.start()

    near_ops, far_ops = near_mat.shape[0], trans.shape[0]
    slot_count = out.shape[1]
    loads[6].wait()
    loads[8].wait()
    loads[9].wait()
    rise.wait()
    fall.wait()
    own_term, highs, lows = [], [], []
    for s in range(species):
        nearby = jnp.concatenate(
            [x.astype(jnp.float32) for x in (before[s], ghosts[0, s], ghosts[1, s], after[s])],
            axis=0,
        ).astype(jnp.bfloat16)
        grouped = jnp.dot(weights[...], nearby, preferred_element_type=jnp.float32)
        own_term.append(grouped[:slot_count])
        high, low = split(grouped[slot_count:])
        highs.append(high)
        lows.append(low)
    total = jnp.concatenate(own_term, axis=0)
    for o in range(near_ops):
        part = slice(o * slot_count, (o + 1) * slot_count)
        stacked = jnp.concatenate(
            [x[part].astype(jnp.float32) for x in highs + lows], axis=0
        ).astype(jnp.bfloat16)
        product = jnp.dot(stacked, near_mat[o], preferred_element_type=jnp.float32)
        total = total + (product[: species * slot_count] + product[species * slot_count :])
    for p in range(1, n):
        there = everyone.at[behind[p]]
        remote(there, there, ex_send.at[p], ex_recv.at[p], "seg", ahead[p]).wait_recv()
    far_rows = []
    for s in range(species):
        source = jnp.concatenate(
            [everyone[e, s * leaf_dev : (s + 1) * leaf_dev, :] for e in range(n)], axis=0
        )
        far_rows.append(jnp.dot(picks[...], source, preferred_element_type=jnp.float32))
    expansion = jnp.zeros((species * slot_count, trans.shape[2]), jnp.float32)
    for o in range(far_ops):
        rows_o = jnp.concatenate(
            [x[o * slot_count : (o + 1) * slot_count] for x in far_rows], axis=0
        ).astype(jnp.bfloat16)
        expansion = expansion + jnp.dot(rows_o, trans[o], preferred_element_type=jnp.float32)
    total = total + jnp.dot(
        expansion.astype(jnp.bfloat16), down[...], preferred_element_type=jnp.float32
    )
    live = table[pl.ds(pl.multiple_of(me * leaf_dev, 8), slot_count), 0:1] == me
    for s in range(species):
        out[s] = jnp.where(live, total[s * slot_count : (s + 1) * slot_count], 0.0)
    for copy in copies:
        copy.wait_send()
    for p in range(1, half):
        there = slots.at[behind[2 * p]]
        remote(there, there, send.at[half + p], recv.at[half + p], "seg", partner).wait_send()


def whole_step(
    coeffs, points, owner_leaf, reaction, fit_matrix, table, near_mat, up_mat, trans_mat,
    down_mat, near_count, far_count,
):
    species, leaf_dev, width = coeffs.shape
    n, n_sp = lax.axis_size("seg"), lax.axis_size("sp")
    blocks = owner_leaf.shape[0]
    count = leaf_dev * blocks
    slots = leaf_dev + 2 * MOVE
    seen = leaf_dev + 2 * (MOVE + REACH)
    half = leaf_dev // 2
    pieces = 3
    f32, bf16, i32 = jnp.float32, jnp.bfloat16, jnp.int32
    dma = pltpu.SemaphoreType.DMA
    return pl.pallas_call(
        functools.partial(step_kernel, n, n_sp, pieces, near_count, far_count),
        out_shape=jax.ShapeDtypeStruct((species, slots, width), f32),
        in_specs=[ANY] * 10,
        out_specs=VMEM,
        scratch_shapes=[
            pltpu.VMEM((n,) + coeffs.shape, f32),
            pltpu.VMEM(points.shape, f32),
            pltpu.SMEM(owner_leaf.shape, i32),
            pltpu.SMEM(reaction.shape, f32),
            pltpu.VMEM(fit_matrix.shape, f32),
            pltpu.VMEM(table.shape, i32),
            pltpu.VMEM(near_mat.shape, bf16),
            pltpu.VMEM(up_mat.shape, bf16),
            pltpu.VMEM(trans_mat.shape, bf16),
            pltpu.VMEM(down_mat.shape, bf16),
            pltpu.VMEM((n * leaf_dev, species * ROWS, 128), f32),
            pltpu.VMEM((3, 16 * count, PB), f32),
            pltpu.VMEM(fit_matrix.shape, bf16),
            pltpu.VMEM(fit_matrix.shape, bf16),
            pltpu.VMEM((n_sp, species, count, PB), f32),
            pltpu.VMEM((2, species, half, width), bf16),
            pltpu.VMEM((species, half, width), bf16),
            pltpu.VMEM((species, half, width), bf16),
            pltpu.VMEM((n, species * leaf_dev, up_mat.shape[0]), bf16),
            pltpu.VMEM(((1 + near_mat.shape[0]) * slots, seen), bf16),
            pltpu.VMEM((far_count * slots, n * leaf_dev), bf16),
            dma((10,)), dma((n,)), dma((n,)), dma((pieces, n_sp)), dma((pieces, n_sp)),
            dma((n + 1,)), dma((n + 1,)),
        ],
        compiler_params=pltpu.CompilerParams(
            collective_id=3, has_side_effects=True, vmem_limit_bytes=LIMIT
        ),
        name="step",
    )(
        coeffs, points, owner_leaf, reaction, fit_matrix, table, near_mat, up_mat, trans_mat,
        down_mat,
    )


def shards(
    coeffs, points, owner_leaf, reaction, fit_matrix, new_seg, near_src, near_op,
    near_mat, up_mat, far_src, trans_mat, down_mat,
):
    species, leaf_dev, width = coeffs.shape
    n = lax.axis_size("seg")
    blocks = owner_leaf.shape[1]
    count = leaf_dev * blocks
    padded_width = -(-width // 128) * 128
    slots = leaf_dev + 2 * MOVE
    table = jnp.concatenate([new_seg[:, None], near_src, near_op, far_src], axis=1)
    table = jnp.pad(table, ((MOVE, MOVE), (0, 0)), constant_values=-1)
    if n * leaf_dev * species * ROWS * 512 <= LIMIT // 2:
        return whole_step(
            coeffs, points, owner_leaf.T, reaction, fit_matrix.T, table, near_mat, up_mat.T,
            trans_mat, down_mat, near_src.shape[1], far_src.shape[1],
        )
    mine = jnp.transpose(coeffs, (1, 0, 2))
    everyone = pair_gather(mine, "seg", 0).reshape(n * leaf_dev, species, width)
    values = pl.pallas_call(
        evaluate_kernel,
        out_shape=jax.ShapeDtypeStruct((species, count, PB), jnp.float32),
        in_specs=[SMEM, VMEM, VMEM],
        out_specs=VMEM,
        scratch_shapes=[
            pltpu.VMEM((8, padded_width), jnp.float32),
            pltpu.VMEM((count * species * ROWS, 128), jnp.float32),
            pltpu.VMEM((3, 16 * count, PB), jnp.float32),
        ],
        compiler_params=pltpu.CompilerParams(vmem_limit_bytes=LIMIT),
        name="evaluate",
    )(owner_leaf, everyone, points)
    gathered = pair_gather(values, "sp", 1)
    half = leaf_dev // 2
    ghosts, equivalent = pl.pallas_call(
        refit_kernel,
        out_shape=(
            jax.ShapeDtypeStruct((2, species, half, width), jnp.bfloat16),
            jax.ShapeDtypeStruct((species * leaf_dev, up_mat.shape[1]), jnp.bfloat16),
        ),
        in_specs=[SMEM, VMEM, VMEM, VMEM, VMEM],
        out_specs=(VMEM, VMEM),
        scratch_shapes=[pltpu.VMEM((species * leaf_dev, blocks * PB), jnp.float32)],
        compiler_params=pltpu.CompilerParams(vmem_limit_bytes=LIMIT),
        name="refit",
    )(reaction, values, gathered, fit_matrix, up_mat)
    before, after, all_equivalent = pl.pallas_call(
        functools.partial(exchange_kernel, n),
        out_shape=(
            jax.ShapeDtypeStruct((species, half, width), jnp.bfloat16),
            jax.ShapeDtypeStruct((species, half, width), jnp.bfloat16),
            jax.ShapeDtypeStruct((n,) + equivalent.shape, jnp.bfloat16),
        ),
        in_specs=[ANY, ANY],
        out_specs=(ANY, ANY, ANY),
        scratch_shapes=[
            pltpu.SemaphoreType.DMA((n + 1,)),
            pltpu.SemaphoreType.DMA((n + 1,)),
            pltpu.SemaphoreType.DMA,
        ],
        compiler_params=pltpu.CompilerParams(collective_id=2, has_side_effects=True),
        name="exchange",
    )(ghosts, equivalent)
    return pl.pallas_call(
        functools.partial(
            finish_kernel, near_count=near_src.shape[1], far_count=far_src.shape[1]
        ),
        out_shape=jax.ShapeDtypeStruct((species, slots, width), jnp.float32),
        in_specs=[VMEM] * 8,
        out_specs=VMEM,
        compiler_params=pltpu.CompilerParams(vmem_limit_bytes=LIMIT),
        name="finish",
    )(table, ghosts, before, after, all_equivalent, near_mat, trans_mat, down_mat)


def solution(mesh):
    placed = (P("sp", "seg", None), P(None, "seg", None), P("seg", None)) + (P(),) * 10
    return jax.shard_map(
        shards, mesh=mesh, in_specs=placed, out_specs=P("sp", "seg", None), check_vma=False
    )
```

```python
import functools

import jax
import jax.numpy as jnp
import numpy as np
from jax import lax
from jax.experimental import pallas as pl
from jax.experimental.pallas import tpu as pltpu
from jax.sharding import PartitionSpec as P

ORDER = 14
PB = 128
MOVE = 4
REACH = 4
MESH = pl.DeviceIdType.MESH
VMEM = pl.BlockSpec(memory_space=pltpu.VMEM)
SMEM = pl.BlockSpec(memory_space=pltpu.SMEM)
ANY = pl.BlockSpec(memory_space=pl.ANY)
LIMIT = 60 * 1024 * 1024


def run_starts():
    starts, counter = {}, 0
    for i in range(ORDER + 1):
        for j in range(ORDER + 1 - i):
            starts[i, j] = counter
            counter += ORDER + 1 - i - j
    return starts, counter


GROUPS = [(i, 0) for i in range(ORDER + 1)] + [(i, 1) for i in range(ORDER + 1 - 8)]
ROWS = 8 * len(GROUPS)


def remote(src, dst, send, recv, axis, to):
    return pltpu.make_async_remote_copy(
        src_ref=src, dst_ref=dst, send_sem=send, recv_sem=recv,
        device_id={axis: to}, device_id_type=MESH,
    )


def greet(axis, others):
    barrier = pltpu.get_barrier_semaphore()
    for to in others:
        pl.semaphore_signal(barrier, inc=1, device_id={axis: to}, device_id_type=MESH)
    pl.semaphore_wait(barrier, len(others))


def pair_gather_kernel(axis, n, src, out, send, recv, local):
    me = lax.axis_index(axis)
    half = n // 2
    partner = me + 1 - 2 * lax.rem(me, 2)
    ahead = [lax.rem(me + 2 * p, n) for p in range(half)]
    behind = [lax.rem(me + n - 2 * p, n) for p in range(half)]
    partner_behind = [lax.rem(partner + n - 2 * p, n) for p in range(half)]
    greet(axis, ahead[1:] + [partner])
    own = pltpu.make_async_copy(src, out.at[me], local)
    own.start()
    copies = []
    for p in range(1, half):
        copies.append(remote(src, out.at[me], send.at[p], recv.at[p], axis, ahead[p]))
        copies[-1].start()
    copies.append(remote(src, out.at[me], send.at[half], recv.at[half], axis, partner))
    copies[-1].start()
    for p in range(1, half):
        slot = out.at[behind[p]]
        remote(slot, slot, send.at[p], recv.at[p], axis, partner).wait_recv()
        copies.append(remote(slot, slot, send.at[half + p], recv.at[half + p], axis, partner))
        copies[-1].start()
    for p in range(half):
        slot = out.at[partner_behind[p]]
        remote(slot, slot, send.at[half + p], recv.at[half + p], axis, partner).wait_recv()
    for copy in copies:
        copy.wait_send()
    own.wait()


def pair_gather(value, axis, collective_id):
    n = lax.axis_size(axis)
    return pl.pallas_call(
        functools.partial(pair_gather_kernel, axis, n),
        out_shape=jax.ShapeDtypeStruct((n,) + value.shape, value.dtype),
        in_specs=[ANY],
        out_specs=ANY,
        scratch_shapes=[
            pltpu.SemaphoreType.DMA((n,)),
            pltpu.SemaphoreType.DMA((n,)),
            pltpu.SemaphoreType.DMA,
        ],
        compiler_params=pltpu.CompilerParams(
            collective_id=collective_id, has_side_effects=True
        ),
        name="gather_" + axis,
    )(value)


def evaluate_kernel(owner, coef, points, values, rows, dense, cheb):
    leaf_dev, blocks = owner.shape
    species = values.shape[0]
    width = coef.shape[2]
    starts, _ = run_starts()
    chunk = 8 // species
    for axis in range(3):
        for m in range(blocks):
            for h in range(leaf_dev // 8):
                x = points[axis, 8 * h : 8 * h + 8, PB * m : PB * m + PB]
                first = 16 * (m * leaf_dev + 8 * h)
                below, here = jnp.ones_like(x), x
                cheb[axis, pl.ds(first, 8, stride=16), :] = below
                for d in range(1, ORDER + 1):
                    cheb[axis, pl.ds(first + d, 8, stride=16), :] = here
                    below, here = here, 2.0 * x * here - below
                cheb[axis, pl.ds(first + ORDER + 1, 8, stride=16), :] = jnp.zeros_like(x)
    lane = lax.broadcasted_iota(jnp.int32, (8, 128), 1)

    def expand(c, carry):
        for k in range(chunk):
            b = c * chunk + k
            leaf = owner[lax.rem(b, leaf_dev), lax.div(b, leaf_dev)]
            rows[species * k : species * (k + 1), :width] = coef[leaf]
        tiles = []
        for t in range(rows.shape[1] // 128):
            x = rows[:, 128 * t : 128 * t + 128]
            x_high = x.astype(jnp.bfloat16).astype(jnp.float32)
            tiles.append((x_high, x - x_high))
        zero = jnp.zeros((8, 128), jnp.float32)
        for g, (i, upper) in enumerate(GROUPS):
            for k in range(8):
                j = 8 * upper + k
                if i + j > ORDER:
                    piece = zero
                else:
                    length = ORDER + 1 - i - j
                    t, shift = divmod(starts[i, j], 128)
                    parts = []
                    for kind in range(2):
                        turn = (128 - shift + 16 * kind) % 128
                        part = tiles[t][kind]
                        if turn:
                            part = pltpu.roll(part, turn, 1)
                        if shift + length > 128:
                            rest = pltpu.roll(tiles[t + 1][kind], turn, 1)
                            part = jnp.where(lane < 128 - shift + 16 * kind, part, rest)
                        parts.append(part)
                    second = jnp.where((lane >= 16) & (lane < 16 + length), parts[1], zero)
                    piece = jnp.where(lane < length, parts[0], second)
                dense[pl.ds(c * (8 * ROWS) + 8 * g + k, 8, stride=ROWS), :] = piece
        return carry

    lax.fori_loop(0, leaf_dev * blocks // chunk, expand, 0)

    def block(b):
        lhs = dense[pl.ds(b * (species * ROWS), species * ROWS), 0:32].astype(jnp.bfloat16)
        tx = cheb[0, pl.ds(b * 16, 16), :]
        ty = cheb[1, pl.ds(b * 16, 16), :]
        tz = cheb[2, pl.ds(b * 16, 16), :]
        high = tz.astype(jnp.bfloat16)
        tz_high = high.astype(jnp.float32)
        rhs = jnp.concatenate(
            [
                jnp.concatenate([tz_high, tz - tz_high], axis=1),
                jnp.concatenate([tz_high, jnp.zeros_like(tz)], axis=1),
            ],
            axis=0,
        ).astype(jnp.bfloat16)
        both = jnp.dot(lhs, rhs, preferred_element_type=jnp.float32)
        inner = both[:, :PB] + both[:, PB:]
        for s in range(species):
            total = [None, None]
            for g, (i, upper) in enumerate(GROUPS):
                r = s * ROWS + 8 * g
                term = inner[r : r + 8] * tx[i : i + 1]
                total[upper] = term if total[upper] is None else total[upper] + term
            summed = total[0] * ty[0:8] + total[1] * ty[8:16]
            values[s, pl.ds(b, 1), :] = jnp.sum(summed, axis=0, keepdims=True)

    def pair(c, carry):
        for k in range(4):
            block(4 * c + k)
        return carry

    lax.fori_loop(0, leaf_dev * blocks // 4, pair, 0)


def split(x):
    high = x.astype(jnp.bfloat16)
    return high, (x - high.astype(jnp.float32)).astype(jnp.bfloat16)


def refit_kernel(reaction, own, gathered, fit, up, ghosts, equivalent, reacted):
    species, block_count, _ = own.shape
    leaf_dev = equivalent.shape[0] // species
    blocks = block_count // leaf_dev
    total_species = reaction.shape[1]
    start = lax.axis_index("sp") * species
    for s in range(species):
        mixing = jnp.zeros((block_count, PB), jnp.float32)
        for r in range(total_species):
            other = gathered[r // species, r % species].astype(jnp.float32)
            mixing = mixing + reaction[start + s, r] * other
        result = own[s] + jnp.tanh(mixing)
        for m in range(blocks):
            reacted[s * leaf_dev : (s + 1) * leaf_dev, m * PB : (m + 1) * PB] = result[
                m * leaf_dev : (m + 1) * leaf_dev
            ]
    high, low = split(reacted[...])
    fit_high, fit_low = split(fit[...])
    main = jnp.dot(
        jnp.concatenate([high, low], axis=0), fit_high, preferred_element_type=jnp.float32
    )
    rest = jnp.dot(high, fit_low, preferred_element_type=jnp.float32)
    count = species * leaf_dev
    refitted = main[:count] + (main[count:] + rest)
    rounded = refitted.astype(jnp.bfloat16)
    half = leaf_dev // 2
    for s in range(species):
        for h in range(2):
            first = s * leaf_dev + h * half
            ghosts[h, s] = refitted[first : first + half].astype(jnp.bfloat16)
    equivalent[...] = jnp.dot(
        rounded, up[...], preferred_element_type=jnp.float32
    ).astype(jnp.bfloat16)


def exchange_kernel(n, ghosts, equivalent, before, after, everyone, send, recv, local):
    me = lax.axis_index("seg")
    ahead = [lax.rem(me + p, n) for p in range(n)]
    behind = [lax.rem(me + n - p, n) for p in range(n)]
    greet("seg", ahead[1:])
    own = pltpu.make_async_copy(equivalent, everyone.at[me], local)
    own.start()
    up = remote(ghosts.at[1], before, send.at[0], recv.at[0], "seg", ahead[1])
    down = remote(ghosts.at[0], after, send.at[n], recv.at[n], "seg", behind[1])
    up.start()
    down.start()
    copies = []
    for p in range(1, n):
        copies.append(
            remote(equivalent, everyone.at[me], send.at[p], recv.at[p], "seg", ahead[p])
        )
        copies[-1].start()
    for p in range(1, n):
        slot = everyone.at[behind[p]]
        remote(slot, slot, send.at[p], recv.at[p], "seg", ahead[p]).wait_recv()
    for copy in copies:
        copy.wait_send()
    up.wait()
    down.wait()
    own.wait()


def finish_kernel(
    table, ghosts, before, after, everyone, near_mat, trans, down, out, near_count, far_count
):
    species, slots, width = out.shape
    half = ghosts.shape[2]
    leaf_dev = 2 * half
    me = lax.axis_index("seg")
    n = everyone.shape[0]
    margin = MOVE + REACH
    near_ops = near_mat.shape[0]
    far_ops = trans.shape[0]
    rows = table[pl.ds(pl.multiple_of(me * leaf_dev, 8), slots), :]
    live = rows[:, 0:1] == me
    base = me * leaf_dev - margin
    seen = leaf_dev + 2 * margin
    near_lane = lax.broadcasted_iota(jnp.int32, (slots, seen), 1)
    slot_row = lax.broadcasted_iota(jnp.int32, (slots, seen), 0)
    near_from = rows[:, 1 : 1 + near_count]
    near_kind = rows[:, 1 + near_count : 1 + 2 * near_count]
    far_from = rows[:, 1 + 2 * near_count : 1 + 2 * near_count + far_count]
    near_from = jnp.where(live & (near_from >= 0), near_from - base, -1)
    far_from = jnp.where(live & (far_from >= 0), far_from, -1)
    weights = [((near_lane == slot_row + REACH) & live).astype(jnp.float32)]
    weights += [jnp.zeros((slots, seen), jnp.float32) for _ in range(near_ops)]
    for q in range(near_count):
        hit = near_lane == near_from[:, q : q + 1]
        for o in range(near_ops):
            chosen = hit & (near_kind[:, q : q + 1] == o)
            weights[1 + o] = weights[1 + o] + chosen.astype(jnp.float32)
    weights = jnp.concatenate(weights, axis=0).astype(jnp.bfloat16)
    leaf_total = n * leaf_dev
    far_lane = lax.broadcasted_iota(jnp.int32, (slots, leaf_total), 1)
    picks = jnp.concatenate(
        [(far_lane == far_from[:, o : o + 1]).astype(jnp.float32) for o in range(far_ops)],
        axis=0,
    ).astype(jnp.bfloat16)
    own_term, highs, lows, far_rows = [], [], [], []
    for s in range(species):
        nearby = jnp.concatenate(
            [x.astype(jnp.float32) for x in (before[s], ghosts[0, s], ghosts[1, s], after[s])],
            axis=0,
        ).astype(jnp.bfloat16)
        grouped = jnp.dot(weights, nearby, preferred_element_type=jnp.float32)
        own_term.append(grouped[:slots])
        high, low = split(grouped[slots:])
        highs.append(high)
        lows.append(low)
        source = jnp.concatenate(
            [everyone[e, s * leaf_dev : (s + 1) * leaf_dev, :] for e in range(n)], axis=0
        )
        far_rows.append(
            jnp.dot(picks, source, preferred_element_type=jnp.float32)
        )
    total = jnp.concatenate(own_term, axis=0)
    for o in range(near_ops):
        part = slice(o * slots, (o + 1) * slots)
        stacked = jnp.concatenate(
            [x[part].astype(jnp.float32) for x in highs + lows], axis=0
        ).astype(jnp.bfloat16)
        product = jnp.dot(stacked, near_mat[o], preferred_element_type=jnp.float32)
        total = total + (product[: species * slots] + product[species * slots :])
    expansion = jnp.zeros((species * slots, trans.shape[2]), jnp.float32)
    for o in range(far_ops):
        rows_o = jnp.concatenate(
            [x[o * slots : (o + 1) * slots] for x in far_rows], axis=0
        ).astype(jnp.bfloat16)
        expansion = expansion + jnp.dot(rows_o, trans[o], preferred_element_type=jnp.float32)
    total = total + jnp.dot(
        expansion.astype(jnp.bfloat16), down[...], preferred_element_type=jnp.float32
    )
    for s in range(species):
        out[s] = jnp.where(live, total[s * slots : (s + 1) * slots], 0.0)


def last_dims(x, y):
    return lax.dot_general(
        x, y, (((1,), (1,)), ((), ())), preferred_element_type=jnp.float32
    )


def step_kernel(
    n, n_sp, pieces, near_count, far_count,
    coeffs, points_in, owner_in, reaction_in, fit_in, table_in, near_in, up_in, trans_in, down_in,
    out,
    slots, points, owner, reaction, fit, table, near_mat, up, trans, down,
    dense, cheb, fit_high, fit_low, gathered, ghosts, before, after, everyone, weights, picks,
    local, send, recv, sp_send, sp_recv, ex_send, ex_recv,
):
    species, leaf_dev, width = coeffs.shape
    blocks = owner.shape[0]
    count = leaf_dev * blocks
    starts, _ = run_starts()
    me = lax.axis_index("seg")
    me_sp = lax.axis_index("sp")
    half = n // 2
    partner = me + 1 - 2 * lax.rem(me, 2)
    ahead = [lax.rem(me + p, n) for p in range(n)]
    behind = [lax.rem(me + n - p, n) for p in range(n)]
    sp_ahead = [lax.rem(me_sp + p, n_sp) for p in range(n_sp)]
    sp_behind = [lax.rem(me_sp + n_sp - p, n_sp) for p in range(n_sp)]

    moves = [
        (coeffs, slots.at[me]), (points_in, points), (owner_in, owner), (reaction_in, reaction),
        (fit_in, fit), (table_in, table), (near_in, near_mat), (up_in, up), (trans_in, trans),
        (down_in, down),
    ]
    loads = [pltpu.make_async_copy(a, b, local.at[k]) for k, (a, b) in enumerate(moves)]
    for load in loads:
        load.start()

    barrier = pltpu.get_barrier_semaphore()
    for to in ahead[1:]:
        pl.semaphore_signal(barrier, inc=1, device_id={"seg": to}, device_id_type=MESH)
    for to in sp_ahead[1:]:
        pl.semaphore_signal(barrier, inc=1, device_id={"sp": to}, device_id_type=MESH)
    pl.semaphore_wait(barrier, n + n_sp - 2)

    copies = []
    for p in range(1, half):
        copies.append(remote(coeffs, slots.at[me], send.at[p], recv.at[p], "seg", ahead[2 * p]))
        copies[-1].start()
    copies.append(remote(coeffs, slots.at[me], send.at[half], recv.at[half], "seg", partner))
    copies[-1].start()

    loads[1].wait()
    for axis in range(3):
        for m in range(blocks):
            for h in range(leaf_dev // 8):
                x = points[axis, 8 * h : 8 * h + 8, PB * m : PB * m + PB]
                first = 16 * (m * leaf_dev + 8 * h)
                prior, here = jnp.ones_like(x), x
                cheb[axis, pl.ds(first, 8, stride=16), :] = prior
                for d in range(1, ORDER + 1):
                    cheb[axis, pl.ds(first + d, 8, stride=16), :] = here
                    prior, here = here, 2.0 * x * here - prior
                cheb[axis, pl.ds(first + ORDER + 1, 8, stride=16), :] = jnp.zeros_like(x)

    lane = lax.broadcasted_iota(jnp.int32, (8, 128), 1)
    zero = jnp.zeros((8, 128), jnp.float32)
    full = width // 128

    def expand(slot):
        def chunk(c, carry):
            s = lax.div(c, leaf_dev // 8)
            h = lax.rem(c, leaf_dev // 8)
            part_rows = pl.ds(pl.multiple_of(8 * h, 8), 8)
            tiles = []
            for t in range(full + (width % 128 > 0)):
                if t < full:
                    x = slots[slot, s, part_rows, 128 * t : 128 * t + 128]
                else:
                    x = slots[slot, s, part_rows, 128 * t : width]
                    x = jnp.concatenate(
                        [x, jnp.zeros((8, 128 - width % 128), jnp.float32)], axis=1
                    )
                x_high = x.astype(jnp.bfloat16).astype(jnp.float32)
                tiles.append((x_high, x - x_high))
            for g, (i, upper) in enumerate(GROUPS):
                turned = []
                for k in range(8):
                    j = 8 * upper + k
                    if i + j > ORDER:
                        piece = zero
                    else:
                        length = ORDER + 1 - i - j
                        t, shift = divmod(starts[i, j], 128)
                        parts = []
                        for kind in range(2):
                            turn = (128 - shift + 16 * kind) % 128
                            part = tiles[t][kind]
                            if turn:
                                part = pltpu.roll(part, turn, 1)
                            if shift + length > 128:
                                rest = pltpu.roll(tiles[t + 1][kind], turn, 1)
                                part = jnp.where(lane < 128 - shift + 16 * kind, part, rest)
                            parts.append(part)
                        second = jnp.where((lane >= 16) & (lane < 16 + length), parts[1], zero)
                        piece = jnp.where(lane < length, parts[0], second)
                    turned.append(piece)
                turned = pltpu.einshape("kln->lkn", jnp.stack(turned, axis=0))
                dense[pl.ds(slot * leaf_dev + 8 * h, 8), pl.ds(pl.multiple_of(s * ROWS + 8 * g, 8), 8), :] = turned
            return carry

        lax.fori_loop(0, species * leaf_dev // 8, chunk, 0)

    loads[0].wait()

    def arrive(p, carry):
        slot = lax.rem(me + n - 2 * p, n)
        other = lax.rem(partner + n - 2 * p, n)

        @pl.when(p > 0)
        def _():
            here = slots.at[slot]
            remote(here, here, send.at[p], recv.at[p], "seg", partner).wait_recv()
            remote(here, here, send.at[half + p], recv.at[half + p], "seg", partner).start()

        expand(slot)
        there = slots.at[other]
        remote(there, there, send.at[half + p], recv.at[half + p], "seg", partner).wait_recv()
        expand(other)

        @pl.when(p == 0)
        def _():
            local_tables()

        return carry

    def local_tables():
        loads[4].wait()
        for k in range(0, fit.shape[0], PB):
            high, low = split(fit[k : min(k + PB, width)])
            fit_high[k : min(k + PB, width)] = high
            fit_low[k : min(k + PB, width)] = low
        loads[5].wait()
        slot_count = out.shape[1]
        rows = table[pl.ds(pl.multiple_of(me * leaf_dev, 8), slot_count), :]
        live = rows[:, 0:1] == me
        margin = MOVE + REACH
        base = me * leaf_dev - margin
        seen = leaf_dev + 2 * margin
        near_lane = lax.broadcasted_iota(jnp.int32, (slot_count, seen), 1)
        slot_row = lax.broadcasted_iota(jnp.int32, (slot_count, seen), 0)
        near_from = rows[:, 1 : 1 + near_count]
        near_kind = rows[:, 1 + near_count : 1 + 2 * near_count]
        far_from = rows[:, 1 + 2 * near_count : 1 + 2 * near_count + far_count]
        near_from = jnp.where(live & (near_from >= 0), near_from - base, -1)
        far_from = jnp.where(live & (far_from >= 0), far_from, -1)
        found = [((near_lane == slot_row + REACH) & live).astype(jnp.float32)]
        found += [jnp.zeros((slot_count, seen), jnp.float32) for _ in range(near_mat.shape[0])]
        for q in range(near_count):
            hit = near_lane == near_from[:, q : q + 1]
            for o in range(near_mat.shape[0]):
                chosen = hit & (near_kind[:, q : q + 1] == o)
                found[1 + o] = found[1 + o] + chosen.astype(jnp.float32)
        weights[...] = jnp.concatenate(found, axis=0).astype(jnp.bfloat16)
        far_lane = lax.broadcasted_iota(jnp.int32, (slot_count, n * leaf_dev), 1)
        picks[...] = jnp.concatenate(
            [(far_lane == far_from[:, o : o + 1]).astype(jnp.float32) for o in range(far_count)],
            axis=0,
        ).astype(jnp.bfloat16)

    lax.fori_loop(0, half, arrive, 0)

    loads[2].wait()

    def block(b):
        leaf = owner[lax.div(b, leaf_dev), lax.rem(b, leaf_dev)]
        lhs = dense[leaf][:, 0:32].astype(jnp.bfloat16)
        here = pl.ds(pl.multiple_of(b * 16, 16), 16)
        tx, ty, tz = cheb[0, here, :], cheb[1, here, :], cheb[2, here, :]
        tz_high = tz.astype(jnp.bfloat16).astype(jnp.float32)
        rhs = jnp.concatenate(
            [
                jnp.concatenate([tz_high, tz - tz_high], axis=1),
                jnp.concatenate([tz_high, jnp.zeros_like(tz)], axis=1),
            ],
            axis=0,
        ).astype(jnp.bfloat16)
        both = jnp.dot(lhs, rhs, preferred_element_type=jnp.float32)
        inner = both[:, :PB] + both[:, PB:]
        for s in range(species):
            total = [None, None]
            for g, (i, upper) in enumerate(GROUPS):
                r = s * ROWS + 8 * g
                term = inner[r : r + 8] * tx[i : i + 1]
                total[upper] = term if total[upper] is None else total[upper] + term
            summed = total[0] * ty[0:8] + total[1] * ty[8:16]
            gathered[me_sp, s, pl.ds(b, 1), :] = jnp.sum(summed, axis=0, keepdims=True)

    step = count // pieces

    def part_of(slot, k):
        return gathered.at[slot, :, step * k : step * (k + 1), :]

    for k in range(pieces):

        def several(c, carry, k=k):
            for u in range(4):
                block(step * k + 4 * c + u)
            return carry

        lax.fori_loop(0, step // 4, several, 0)
        mine = part_of(me_sp, k)
        for p in range(1, n_sp):
            copies.append(
                remote(mine, mine, sp_send.at[k, p], sp_recv.at[k, p], "sp", sp_ahead[p])
            )
            copies[-1].start()

    loads[3].wait()
    rows_total = species * leaf_dev
    refitted = jnp.zeros((rows_total, width), jnp.float32)
    per = step // leaf_dev
    for k in range(pieces):
        for p in range(1, n_sp):
            there = part_of(sp_behind[p], k)
            remote(there, there, sp_send.at[k, p], sp_recv.at[k, p], "sp", sp_ahead[p]).wait_recv()
        by_species = []
        for s in range(species):
            mixing = jnp.zeros((step, PB), jnp.float32)
            for r in range(n_sp * species):
                other = gathered[r // species, r % species, step * k : step * (k + 1), :]
                mixing = mixing + reaction[me_sp * species + s, r] * other
            by_species.append(
                gathered[me_sp, s, step * k : step * (k + 1), :] + jnp.tanh(mixing)
            )
        reacted = jnp.concatenate(
            [
                jnp.concatenate(
                    [x[m * leaf_dev : (m + 1) * leaf_dev] for x in by_species], axis=0
                )
                for m in range(per)
            ],
            axis=1,
        )
        high, low = split(reacted)
        nodes = slice(k * per * PB, (k + 1) * per * PB)
        main = last_dims(jnp.concatenate([high, low], axis=0), fit_high[:, nodes])
        rest = last_dims(high, fit_low[:, nodes])
        refitted = refitted + (main[:rows_total] + (main[rows_total:] + rest))
    rounded = refitted.astype(jnp.bfloat16)
    half_leaf = leaf_dev // 2
    for s in range(species):
        for h in range(2):
            first = s * leaf_dev + h * half_leaf
            ghosts[h, s] = refitted[first : first + half_leaf].astype(jnp.bfloat16)
    rise = remote(ghosts.at[1], before, ex_send.at[0], ex_recv.at[0], "seg", ahead[1])
    fall = remote(ghosts.at[0], after, ex_send.at[n], ex_recv.at[n], "seg", behind[1])
    loads[7].wait()
    everyone[me] = last_dims(rounded, up[...]).astype(jnp.bfloat16)
    for p in range(1, n):
        mine = everyone.at[me]
        copies.append(remote(mine, mine, ex_send.at[p], ex_recv.at[p], "seg", ahead[p]))
        copies[-1].start()
    rise.start()
    fall.start()

    near_ops, far_ops = near_mat.shape[0], trans.shape[0]
    slot_count = out.shape[1]
    loads[6].wait()
    loads[8].wait()
    loads[9].wait()
    rise.wait()
    fall.wait()
    own_term, highs, lows = [], [], []
    for s in range(species):
        nearby = jnp.concatenate(
            [x.astype(jnp.float32) for x in (before[s], ghosts[0, s], ghosts[1, s], after[s])],
            axis=0,
        ).astype(jnp.bfloat16)
        grouped = jnp.dot(weights[...], nearby, preferred_element_type=jnp.float32)
        own_term.append(grouped[:slot_count])
        high, low = split(grouped[slot_count:])
        highs.append(high)
        lows.append(low)
    total = jnp.concatenate(own_term, axis=0)
    for o in range(near_ops):
        part = slice(o * slot_count, (o + 1) * slot_count)
        stacked = jnp.concatenate(
            [x[part].astype(jnp.float32) for x in highs + lows], axis=0
        ).astype(jnp.bfloat16)
        product = jnp.dot(stacked, near_mat[o], preferred_element_type=jnp.float32)
        total = total + (product[: species * slot_count] + product[species * slot_count :])
    for p in range(1, n):
        there = everyone.at[behind[p]]
        remote(there, there, ex_send.at[p], ex_recv.at[p], "seg", ahead[p]).wait_recv()
    far_rows = []
    for s in range(species):
        source = jnp.concatenate(
            [everyone[e, s * leaf_dev : (s + 1) * leaf_dev, :] for e in range(n)], axis=0
        )
        far_rows.append(jnp.dot(picks[...], source, preferred_element_type=jnp.float32))
    expansion = jnp.zeros((species * slot_count, trans.shape[2]), jnp.float32)
    for o in range(far_ops):
        rows_o = jnp.concatenate(
            [x[o * slot_count : (o + 1) * slot_count] for x in far_rows], axis=0
        ).astype(jnp.bfloat16)
        expansion = expansion + jnp.dot(rows_o, trans[o], preferred_element_type=jnp.float32)
    total = total + jnp.dot(
        expansion.astype(jnp.bfloat16), down[...], preferred_element_type=jnp.float32
    )
    live = table[pl.ds(pl.multiple_of(me * leaf_dev, 8), slot_count), 0:1] == me
    for s in range(species):
        out[s] = jnp.where(live, total[s * slot_count : (s + 1) * slot_count], 0.0)
    for copy in copies:
        copy.wait_send()
    for p in range(1, half):
        there = slots.at[behind[2 * p]]
        remote(there, there, send.at[half + p], recv.at[half + p], "seg", partner).wait_send()


def whole_step(
    coeffs, points, owner_leaf, reaction, fit_matrix, table, near_mat, up_mat, trans_mat,
    down_mat, near_count, far_count,
):
    species, leaf_dev, width = coeffs.shape
    n, n_sp = lax.axis_size("seg"), lax.axis_size("sp")
    blocks = owner_leaf.shape[0]
    count = leaf_dev * blocks
    slots = leaf_dev + 2 * MOVE
    seen = leaf_dev + 2 * (MOVE + REACH)
    half = leaf_dev // 2
    pieces = 3
    f32, bf16, i32 = jnp.float32, jnp.bfloat16, jnp.int32
    dma = pltpu.SemaphoreType.DMA
    return pl.pallas_call(
        functools.partial(step_kernel, n, n_sp, pieces, near_count, far_count),
        out_shape=jax.ShapeDtypeStruct((species, slots, width), f32),
        in_specs=[ANY] * 10,
        out_specs=VMEM,
        scratch_shapes=[
            pltpu.VMEM((n,) + coeffs.shape, f32),
            pltpu.VMEM(points.shape, f32),
            pltpu.SMEM(owner_leaf.shape, i32),
            pltpu.SMEM(reaction.shape, f32),
            pltpu.VMEM(fit_matrix.shape, f32),
            pltpu.VMEM(table.shape, i32),
            pltpu.VMEM(near_mat.shape, bf16),
            pltpu.VMEM(up_mat.shape, bf16),
            pltpu.VMEM(trans_mat.shape, bf16),
            pltpu.VMEM(down_mat.shape, bf16),
            pltpu.VMEM((n * leaf_dev, species * ROWS, 128), f32),
            pltpu.VMEM((3, 16 * count, PB), f32),
            pltpu.VMEM(fit_matrix.shape, bf16),
            pltpu.VMEM(fit_matrix.shape, bf16),
            pltpu.VMEM((n_sp, species, count, PB), f32),
            pltpu.VMEM((2, species, half, width), bf16),
            pltpu.VMEM((species, half, width), bf16),
            pltpu.VMEM((species, half, width), bf16),
            pltpu.VMEM((n, species * leaf_dev, up_mat.shape[0]), bf16),
            pltpu.VMEM(((1 + near_mat.shape[0]) * slots, seen), bf16),
            pltpu.VMEM((far_count * slots, n * leaf_dev), bf16),
            dma((10,)), dma((n,)), dma((n,)), dma((pieces, n_sp)), dma((pieces, n_sp)),
            dma((n + 1,)), dma((n + 1,)),
        ],
        compiler_params=pltpu.CompilerParams(
            collective_id=3, has_side_effects=True, vmem_limit_bytes=LIMIT
        ),
        name="step",
    )(
        coeffs, points, owner_leaf, reaction, fit_matrix, table, near_mat, up_mat, trans_mat,
        down_mat,
    )


def shards(
    coeffs, points, owner_leaf, reaction, fit_matrix, new_seg, near_src, near_op,
    near_mat, up_mat, far_src, trans_mat, down_mat,
):
    species, leaf_dev, width = coeffs.shape
    n = lax.axis_size("seg")
    blocks = owner_leaf.shape[1]
    count = leaf_dev * blocks
    padded_width = -(-width // 128) * 128
    slots = leaf_dev + 2 * MOVE
    table = jnp.concatenate([new_seg[:, None], near_src, near_op, far_src], axis=1)
    table = jnp.pad(table, ((MOVE, MOVE), (0, 0)), constant_values=-1)
    if n * leaf_dev * species * ROWS * 512 <= LIMIT // 2:
        return whole_step(
            coeffs, points, owner_leaf.T, reaction, fit_matrix.T, table, near_mat, up_mat.T,
            trans_mat, down_mat, near_src.shape[1], far_src.shape[1],
        )
    mine = jnp.transpose(coeffs, (1, 0, 2))
    everyone = pair_gather(mine, "seg", 0).reshape(n * leaf_dev, species, width)
    values = pl.pallas_call(
        evaluate_kernel,
        out_shape=jax.ShapeDtypeStruct((species, count, PB), jnp.float32),
        in_specs=[SMEM, VMEM, VMEM],
        out_specs=VMEM,
        scratch_shapes=[
            pltpu.VMEM((8, padded_width), jnp.float32),
            pltpu.VMEM((count * species * ROWS, 128), jnp.float32),
            pltpu.VMEM((3, 16 * count, PB), jnp.float32),
        ],
        compiler_params=pltpu.CompilerParams(vmem_limit_bytes=LIMIT),
        name="evaluate",
    )(owner_leaf, everyone, points)
    gathered = pair_gather(values, "sp", 1)
    half = leaf_dev // 2
    ghosts, equivalent = pl.pallas_call(
        refit_kernel,
        out_shape=(
            jax.ShapeDtypeStruct((2, species, half, width), jnp.bfloat16),
            jax.ShapeDtypeStruct((species * leaf_dev, up_mat.shape[1]), jnp.bfloat16),
        ),
        in_specs=[SMEM, VMEM, VMEM, VMEM, VMEM],
        out_specs=(VMEM, VMEM),
        scratch_shapes=[pltpu.VMEM((species * leaf_dev, blocks * PB), jnp.float32)],
        compiler_params=pltpu.CompilerParams(vmem_limit_bytes=LIMIT),
        name="refit",
    )(reaction, values, gathered, fit_matrix, up_mat)
    before, after, all_equivalent = pl.pallas_call(
        functools.partial(exchange_kernel, n),
        out_shape=(
            jax.ShapeDtypeStruct((species, half, width), jnp.bfloat16),
            jax.ShapeDtypeStruct((species, half, width), jnp.bfloat16),
            jax.ShapeDtypeStruct((n,) + equivalent.shape, jnp.bfloat16),
        ),
        in_specs=[ANY, ANY],
        out_specs=(ANY, ANY, ANY),
        scratch_shapes=[
            pltpu.SemaphoreType.DMA((n + 1,)),
            pltpu.SemaphoreType.DMA((n + 1,)),
            pltpu.SemaphoreType.DMA,
        ],
        compiler_params=pltpu.CompilerParams(collective_id=2, has_side_effects=True),
        name="exchange",
    )(ghosts, equivalent)
    return pl.pallas_call(
        functools.partial(
            finish_kernel, near_count=near_src.shape[1], far_count=far_src.shape[1]
        ),
        out_shape=jax.ShapeDtypeStruct((species, slots, width), jnp.float32),
        in_specs=[VMEM] * 8,
        out_specs=VMEM,
        compiler_params=pltpu.CompilerParams(vmem_limit_bytes=LIMIT),
        name="finish",
    )(table, ghosts, before, after, all_equivalent, near_mat, trans_mat, down_mat)


def solution(mesh):
    placed = (P("sp", "seg", None), P(None, "seg", None), P("seg", None)) + (P(),) * 10
    return jax.shard_map(
        shards, mesh=mesh, in_specs=placed, out_specs=P("sp", "seg", None), check_vma=False
    )
```

```python
import functools

import jax
import jax.numpy as jnp
import numpy as np
from jax import lax
from jax.experimental import pallas as pl
from jax.experimental.pallas import tpu as pltpu
from jax.sharding import PartitionSpec as P

ORDER = 14
PB = 128
MOVE = 4
REACH = 4
MESH = pl.DeviceIdType.MESH
VMEM = pl.BlockSpec(memory_space=pltpu.VMEM)
SMEM = pl.BlockSpec(memory_space=pltpu.SMEM)
ANY = pl.BlockSpec(memory_space=pl.ANY)
LIMIT = 60 * 1024 * 1024


def run_starts():
    starts, counter = {}, 0
    for i in range(ORDER + 1):
        for j in range(ORDER + 1 - i):
            starts[i, j] = counter
            counter += ORDER + 1 - i - j
    return starts, counter


GROUPS = [(i, 0) for i in range(ORDER + 1)] + [(i, 1) for i in range(ORDER + 1 - 8)]
ROWS = 8 * len(GROUPS)


def remote(src, dst, send, recv, axis, to):
    return pltpu.make_async_remote_copy(
        src_ref=src, dst_ref=dst, send_sem=send, recv_sem=recv,
        device_id={axis: to}, device_id_type=MESH,
    )


def greet(axis, others):
    barrier = pltpu.get_barrier_semaphore()
    for to in others:
        pl.semaphore_signal(barrier, inc=1, device_id={axis: to}, device_id_type=MESH)
    pl.semaphore_wait(barrier, len(others))


def pair_gather_kernel(axis, n, src, out, send, recv, local):
    me = lax.axis_index(axis)
    half = n // 2
    partner = me + 1 - 2 * lax.rem(me, 2)
    ahead = [lax.rem(me + 2 * p, n) for p in range(half)]
    behind = [lax.rem(me + n - 2 * p, n) for p in range(half)]
    partner_behind = [lax.rem(partner + n - 2 * p, n) for p in range(half)]
    greet(axis, ahead[1:] + [partner])
    own = pltpu.make_async_copy(src, out.at[me], local)
    own.start()
    copies = []
    for p in range(1, half):
        copies.append(remote(src, out.at[me], send.at[p], recv.at[p], axis, ahead[p]))
        copies[-1].start()
    copies.append(remote(src, out.at[me], send.at[half], recv.at[half], axis, partner))
    copies[-1].start()
    for p in range(1, half):
        slot = out.at[behind[p]]
        remote(slot, slot, send.at[p], recv.at[p], axis, partner).wait_recv()
        copies.append(remote(slot, slot, send.at[half + p], recv.at[half + p], axis, partner))
        copies[-1].start()
    for p in range(half):
        slot = out.at[partner_behind[p]]
        remote(slot, slot, send.at[half + p], recv.at[half + p], axis, partner).wait_recv()
    for copy in copies:
        copy.wait_send()
    own.wait()


def pair_gather(value, axis, collective_id):
    n = lax.axis_size(axis)
    return pl.pallas_call(
        functools.partial(pair_gather_kernel, axis, n),
        out_shape=jax.ShapeDtypeStruct((n,) + value.shape, value.dtype),
        in_specs=[ANY],
        out_specs=ANY,
        scratch_shapes=[
            pltpu.SemaphoreType.DMA((n,)),
            pltpu.SemaphoreType.DMA((n,)),
            pltpu.SemaphoreType.DMA,
        ],
        compiler_params=pltpu.CompilerParams(
            collective_id=collective_id, has_side_effects=True
        ),
        name="gather_" + axis,
    )(value)


def evaluate_kernel(owner, coef, points, values, rows, dense, cheb):
    leaf_dev, blocks = owner.shape
    species = values.shape[0]
    width = coef.shape[2]
    starts, _ = run_starts()
    chunk = 8 // species
    for axis in range(3):
        for m in range(blocks):
            for h in range(leaf_dev // 8):
                x = points[axis, 8 * h : 8 * h + 8, PB * m : PB * m + PB]
                first = 16 * (m * leaf_dev + 8 * h)
                below, here = jnp.ones_like(x), x
                cheb[axis, pl.ds(first, 8, stride=16), :] = below
                for d in range(1, ORDER + 1):
                    cheb[axis, pl.ds(first + d, 8, stride=16), :] = here
                    below, here = here, 2.0 * x * here - below
                cheb[axis, pl.ds(first + ORDER + 1, 8, stride=16), :] = jnp.zeros_like(x)
    lane = lax.broadcasted_iota(jnp.int32, (8, 128), 1)

    def expand(c, carry):
        for k in range(chunk):
            b = c * chunk + k
            leaf = owner[lax.rem(b, leaf_dev), lax.div(b, leaf_dev)]
            rows[species * k : species * (k + 1), :width] = coef[leaf]
        tiles = []
        for t in range(rows.shape[1] // 128):
            x = rows[:, 128 * t : 128 * t + 128]
            x_high = x.astype(jnp.bfloat16).astype(jnp.float32)
            tiles.append((x_high, x - x_high))
        zero = jnp.zeros((8, 128), jnp.float32)
        for g, (i, upper) in enumerate(GROUPS):
            for k in range(8):
                j = 8 * upper + k
                if i + j > ORDER:
                    piece = zero
                else:
                    length = ORDER + 1 - i - j
                    t, shift = divmod(starts[i, j], 128)
                    parts = []
                    for kind in range(2):
                        turn = (128 - shift + 16 * kind) % 128
                        part = tiles[t][kind]
                        if turn:
                            part = pltpu.roll(part, turn, 1)
                        if shift + length > 128:
                            rest = pltpu.roll(tiles[t + 1][kind], turn, 1)
                            part = jnp.where(lane < 128 - shift + 16 * kind, part, rest)
                        parts.append(part)
                    second = jnp.where((lane >= 16) & (lane < 16 + length), parts[1], zero)
                    piece = jnp.where(lane < length, parts[0], second)
                dense[pl.ds(c * (8 * ROWS) + 8 * g + k, 8, stride=ROWS), :] = piece
        return carry

    lax.fori_loop(0, leaf_dev * blocks // chunk, expand, 0)

    def block(b):
        lhs = dense[pl.ds(b * (species * ROWS), species * ROWS), 0:32].astype(jnp.bfloat16)
        tx = cheb[0, pl.ds(b * 16, 16), :]
        ty = cheb[1, pl.ds(b * 16, 16), :]
        tz = cheb[2, pl.ds(b * 16, 16), :]
        high = tz.astype(jnp.bfloat16)
        tz_high = high.astype(jnp.float32)
        rhs = jnp.concatenate(
            [
                jnp.concatenate([tz_high, tz - tz_high], axis=1),
                jnp.concatenate([tz_high, jnp.zeros_like(tz)], axis=1),
            ],
            axis=0,
        ).astype(jnp.bfloat16)
        both = jnp.dot(lhs, rhs, preferred_element_type=jnp.float32)
        inner = both[:, :PB] + both[:, PB:]
        for s in range(species):
            total = [None, None]
            for g, (i, upper) in enumerate(GROUPS):
                r = s * ROWS + 8 * g
                term = inner[r : r + 8] * tx[i : i + 1]
                total[upper] = term if total[upper] is None else total[upper] + term
            summed = total[0] * ty[0:8] + total[1] * ty[8:16]
            values[s, pl.ds(b, 1), :] = jnp.sum(summed, axis=0, keepdims=True)

    def pair(c, carry):
        for k in range(4):
            block(4 * c + k)
        return carry

    lax.fori_loop(0, leaf_dev * blocks // 4, pair, 0)


def split(x):
    high = x.astype(jnp.bfloat16)
    return high, (x - high.astype(jnp.float32)).astype(jnp.bfloat16)


def refit_kernel(reaction, own, gathered, fit, up, ghosts, equivalent, reacted):
    species, block_count, _ = own.shape
    leaf_dev = equivalent.shape[0] // species
    blocks = block_count // leaf_dev
    total_species = reaction.shape[1]
    start = lax.axis_index("sp") * species
    for s in range(species):
        mixing = jnp.zeros((block_count, PB), jnp.float32)
        for r in range(total_species):
            other = gathered[r // species, r % species].astype(jnp.float32)
            mixing = mixing + reaction[start + s, r] * other
        result = own[s] + jnp.tanh(mixing)
        for m in range(blocks):
            reacted[s * leaf_dev : (s + 1) * leaf_dev, m * PB : (m + 1) * PB] = result[
                m * leaf_dev : (m + 1) * leaf_dev
            ]
    high, low = split(reacted[...])
    fit_high, fit_low = split(fit[...])
    main = jnp.dot(
        jnp.concatenate([high, low], axis=0), fit_high, preferred_element_type=jnp.float32
    )
    rest = jnp.dot(high, fit_low, preferred_element_type=jnp.float32)
    count = species * leaf_dev
    refitted = main[:count] + (main[count:] + rest)
    rounded = refitted.astype(jnp.bfloat16)
    half = leaf_dev // 2
    for s in range(species):
        for h in range(2):
            first = s * leaf_dev + h * half
            ghosts[h, s] = refitted[first : first + half].astype(jnp.bfloat16)
    equivalent[...] = jnp.dot(
        rounded, up[...], preferred_element_type=jnp.float32
    ).astype(jnp.bfloat16)


def exchange_kernel(n, ghosts, equivalent, before, after, everyone, send, recv, local):
    me = lax.axis_index("seg")
    ahead = [lax.rem(me + p, n) for p in range(n)]
    behind = [lax.rem(me + n - p, n) for p in range(n)]
    greet("seg", ahead[1:])
    own = pltpu.make_async_copy(equivalent, everyone.at[me], local)
    own.start()
    up = remote(ghosts.at[1], before, send.at[0], recv.at[0], "seg", ahead[1])
    down = remote(ghosts.at[0], after, send.at[n], recv.at[n], "seg", behind[1])
    up.start()
    down.start()
    copies = []
    for p in range(1, n):
        copies.append(
            remote(equivalent, everyone.at[me], send.at[p], recv.at[p], "seg", ahead[p])
        )
        copies[-1].start()
    for p in range(1, n):
        slot = everyone.at[behind[p]]
        remote(slot, slot, send.at[p], recv.at[p], "seg", ahead[p]).wait_recv()
    for copy in copies:
        copy.wait_send()
    up.wait()
    down.wait()
    own.wait()


def finish_kernel(
    table, ghosts, before, after, everyone, near_mat, trans, down, out, near_count, far_count
):
    species, slots, width = out.shape
    half = ghosts.shape[2]
    leaf_dev = 2 * half
    me = lax.axis_index("seg")
    n = everyone.shape[0]
    margin = MOVE + REACH
    near_ops = near_mat.shape[0]
    far_ops = trans.shape[0]
    rows = table[pl.ds(pl.multiple_of(me * leaf_dev, 8), slots), :]
    live = rows[:, 0:1] == me
    base = me * leaf_dev - margin
    seen = leaf_dev + 2 * margin
    near_lane = lax.broadcasted_iota(jnp.int32, (slots, seen), 1)
    slot_row = lax.broadcasted_iota(jnp.int32, (slots, seen), 0)
    near_from = rows[:, 1 : 1 + near_count]
    near_kind = rows[:, 1 + near_count : 1 + 2 * near_count]
    far_from = rows[:, 1 + 2 * near_count : 1 + 2 * near_count + far_count]
    near_from = jnp.where(live & (near_from >= 0), near_from - base, -1)
    far_from = jnp.where(live & (far_from >= 0), far_from, -1)
    weights = [((near_lane == slot_row + REACH) & live).astype(jnp.float32)]
    weights += [jnp.zeros((slots, seen), jnp.float32) for _ in range(near_ops)]
    for q in range(near_count):
        hit = near_lane == near_from[:, q : q + 1]
        for o in range(near_ops):
            chosen = hit & (near_kind[:, q : q + 1] == o)
            weights[1 + o] = weights[1 + o] + chosen.astype(jnp.float32)
    weights = jnp.concatenate(weights, axis=0).astype(jnp.bfloat16)
    leaf_total = n * leaf_dev
    far_lane = lax.broadcasted_iota(jnp.int32, (slots, leaf_total), 1)
    picks = jnp.concatenate(
        [(far_lane == far_from[:, o : o + 1]).astype(jnp.float32) for o in range(far_ops)],
        axis=0,
    ).astype(jnp.bfloat16)
    own_term, highs, lows, far_rows = [], [], [], []
    for s in range(species):
        nearby = jnp.concatenate(
            [x.astype(jnp.float32) for x in (before[s], ghosts[0, s], ghosts[1, s], after[s])],
            axis=0,
        ).astype(jnp.bfloat16)
        grouped = jnp.dot(weights, nearby, preferred_element_type=jnp.float32)
        own_term.append(grouped[:slots])
        high, low = split(grouped[slots:])
        highs.append(high)
        lows.append(low)
        source = jnp.concatenate(
            [everyone[e, s * leaf_dev : (s + 1) * leaf_dev, :] for e in range(n)], axis=0
        )
        far_rows.append(
            jnp.dot(picks, source, preferred_element_type=jnp.float32)
        )
    total = jnp.concatenate(own_term, axis=0)
    for o in range(near_ops):
        part = slice(o * slots, (o + 1) * slots)
        stacked = jnp.concatenate(
            [x[part].astype(jnp.float32) for x in highs + lows], axis=0
        ).astype(jnp.bfloat16)
        product = jnp.dot(stacked, near_mat[o], preferred_element_type=jnp.float32)
        total = total + (product[: species * slots] + product[species * slots :])
    expansion = jnp.zeros((species * slots, trans.shape[2]), jnp.float32)
    for o in range(far_ops):
        rows_o = jnp.concatenate(
            [x[o * slots : (o + 1) * slots] for x in far_rows], axis=0
        ).astype(jnp.bfloat16)
        expansion = expansion + jnp.dot(rows_o, trans[o], preferred_element_type=jnp.float32)
    total = total + jnp.dot(
        expansion.astype(jnp.bfloat16), down[...], preferred_element_type=jnp.float32
    )
    for s in range(species):
        out[s] = jnp.where(live, total[s * slots : (s + 1) * slots], 0.0)


def last_dims(x, y):
    return lax.dot_general(
        x, y, (((1,), (1,)), ((), ())), preferred_element_type=jnp.float32
    )


def step_kernel(
    n, n_sp, pieces, near_count, far_count,
    coeffs, points_in, owner_in, reaction_in, fit_in, table_in, near_in, up_in, trans_in, down_in,
    out,
    slots, points, owner, reaction, fit, table, near_mat, up, trans, down,
    dense, cheb, fit_high, fit_low, gathered, ghosts, before, after, everyone, weights, picks,
    local, send, recv, sp_send, sp_recv, ex_send, ex_recv,
):
    species, leaf_dev, width = coeffs.shape
    blocks = owner.shape[0]
    count = leaf_dev * blocks
    starts, _ = run_starts()
    me = lax.axis_index("seg")
    me_sp = lax.axis_index("sp")
    half = n // 2
    partner = me + 1 - 2 * lax.rem(me, 2)
    ahead = [lax.rem(me + p, n) for p in range(n)]
    behind = [lax.rem(me + n - p, n) for p in range(n)]
    sp_ahead = [lax.rem(me_sp + p, n_sp) for p in range(n_sp)]
    sp_behind = [lax.rem(me_sp + n_sp - p, n_sp) for p in range(n_sp)]

    moves = [
        (coeffs, slots.at[me]), (points_in, points), (owner_in, owner), (reaction_in, reaction),
        (fit_in, fit), (table_in, table), (near_in, near_mat), (up_in, up), (trans_in, trans),
        (down_in, down),
    ]
    loads = [pltpu.make_async_copy(a, b, local.at[k]) for k, (a, b) in enumerate(moves)]
    for load in loads:
        load.start()

    barrier = pltpu.get_barrier_semaphore()
    for to in ahead[1:]:
        pl.semaphore_signal(barrier, inc=1, device_id={"seg": to}, device_id_type=MESH)
    for to in sp_ahead[1:]:
        pl.semaphore_signal(barrier, inc=1, device_id={"sp": to}, device_id_type=MESH)
    pl.semaphore_wait(barrier, n + n_sp - 2)

    copies = []
    for p in range(1, half):
        copies.append(remote(coeffs, slots.at[me], send.at[p], recv.at[p], "seg", ahead[2 * p]))
        copies[-1].start()
    copies.append(remote(coeffs, slots.at[me], send.at[half], recv.at[half], "seg", partner))
    copies[-1].start()

    loads[1].wait()
    for axis in range(3):
        for m in range(blocks):
            for h in range(leaf_dev // 8):
                x = points[axis, 8 * h : 8 * h + 8, PB * m : PB * m + PB]
                first = 16 * (m * leaf_dev + 8 * h)
                prior, here = jnp.ones_like(x), x
                cheb[axis, pl.ds(first, 8, stride=16), :] = prior
                for d in range(1, ORDER + 1):
                    cheb[axis, pl.ds(first + d, 8, stride=16), :] = here
                    prior, here = here, 2.0 * x * here - prior
                cheb[axis, pl.ds(first + ORDER + 1, 8, stride=16), :] = jnp.zeros_like(x)

    lane = lax.broadcasted_iota(jnp.int32, (8, 128), 1)
    zero = jnp.zeros((8, 128), jnp.float32)
    full = width // 128

    def expand(slot):
        def chunk(c, carry):
            s = lax.div(c, leaf_dev // 8)
            h = lax.rem(c, leaf_dev // 8)
            part_rows = pl.ds(pl.multiple_of(8 * h, 8), 8)
            tiles = []
            for t in range(full + (width % 128 > 0)):
                if t < full:
                    x = slots[slot, s, part_rows, 128 * t : 128 * t + 128]
                else:
                    x = slots[slot, s, part_rows, 128 * t : width]
                    x = jnp.concatenate(
                        [x, jnp.zeros((8, 128 - width % 128), jnp.float32)], axis=1
                    )
                x_high = x.astype(jnp.bfloat16).astype(jnp.float32)
                tiles.append((x_high, x - x_high))
            for g, (i, upper) in enumerate(GROUPS):
                turned = []
                for k in range(8):
                    j = 8 * upper + k
                    if i + j > ORDER:
                        piece = zero
                    else:
                        length = ORDER + 1 - i - j
                        t, shift = divmod(starts[i, j], 128)
                        parts = []
                        for kind in range(3):
                            turn = (128 - shift + 16 * kind) % 128
                            part = tiles[t][kind % 2]
                            if turn:
                                part = pltpu.roll(part, turn, 1)
                            if shift + length > 128:
                                rest = pltpu.roll(tiles[t + 1][kind % 2], turn, 1)
                                part = jnp.where(lane < 128 - shift + 16 * kind, part, rest)
                            parts.append(part)
                        third = jnp.where((lane >= 32) & (lane < 32 + length), parts[2], zero)
                        second = jnp.where((lane >= 16) & (lane < 16 + length), parts[1], third)
                        piece = jnp.where(lane < length, parts[0], second)
                    turned.append(piece)
                turned = pltpu.einshape("kln->lkn", jnp.stack(turned, axis=0))
                dense[pl.ds(slot * leaf_dev + 8 * h, 8), pl.ds(pl.multiple_of(s * ROWS + 8 * g, 8), 8), :] = turned
            return carry

        lax.fori_loop(0, species * leaf_dev // 8, chunk, 0)

    loads[0].wait()

    def arrive(p, carry):
        slot = lax.rem(me + n - 2 * p, n)
        other = lax.rem(partner + n - 2 * p, n)

        @pl.when(p > 0)
        def _():
            here = slots.at[slot]
            remote(here, here, send.at[p], recv.at[p], "seg", partner).wait_recv()
            remote(here, here, send.at[half + p], recv.at[half + p], "seg", partner).start()

        expand(slot)
        there = slots.at[other]
        remote(there, there, send.at[half + p], recv.at[half + p], "seg", partner).wait_recv()
        expand(other)

        @pl.when(p == 0)
        def _():
            local_tables()

        return carry

    def local_tables():
        loads[4].wait()
        for k in range(0, fit.shape[0], PB):
            high, low = split(fit[k : min(k + PB, width)])
            fit_high[k : min(k + PB, width)] = high
            fit_low[k : min(k + PB, width)] = low
        loads[5].wait()
        slot_count = out.shape[1]
        rows = table[pl.ds(pl.multiple_of(me * leaf_dev, 8), slot_count), :]
        live = rows[:, 0:1] == me
        margin = MOVE + REACH
        base = me * leaf_dev - margin
        seen = leaf_dev + 2 * margin
        near_lane = lax.broadcasted_iota(jnp.int32, (slot_count, seen), 1)
        slot_row = lax.broadcasted_iota(jnp.int32, (slot_count, seen), 0)
        near_from = rows[:, 1 : 1 + near_count]
        near_kind = rows[:, 1 + near_count : 1 + 2 * near_count]
        far_from = rows[:, 1 + 2 * near_count : 1 + 2 * near_count + far_count]
        near_from = jnp.where(live & (near_from >= 0), near_from - base, -1)
        far_from = jnp.where(live & (far_from >= 0), far_from, -1)
        found = [((near_lane == slot_row + REACH) & live).astype(jnp.float32)]
        found += [jnp.zeros((slot_count, seen), jnp.float32) for _ in range(near_mat.shape[0])]
        for q in range(near_count):
            hit = near_lane == near_from[:, q : q + 1]
            for o in range(near_mat.shape[0]):
                chosen = hit & (near_kind[:, q : q + 1] == o)
                found[1 + o] = found[1 + o] + chosen.astype(jnp.float32)
        weights[...] = jnp.concatenate(found, axis=0).astype(jnp.bfloat16)
        far_lane = lax.broadcasted_iota(jnp.int32, (slot_count, n * leaf_dev), 1)
        picks[...] = jnp.concatenate(
            [(far_lane == far_from[:, o : o + 1]).astype(jnp.float32) for o in range(far_count)],
            axis=0,
        ).astype(jnp.bfloat16)

    lax.fori_loop(0, half, arrive, 0)

    loads[2].wait()

    def block(b):
        leaf = owner[lax.div(b, leaf_dev), lax.rem(b, leaf_dev)]
        lhs = dense[leaf][:, 0:48].astype(jnp.bfloat16)
        here = pl.ds(pl.multiple_of(b * 16, 16), 16)
        tx, ty, tz = cheb[0, here, :], cheb[1, here, :], cheb[2, here, :]
        tz_high = tz.astype(jnp.bfloat16).astype(jnp.float32)
        rhs = jnp.concatenate([tz_high, tz_high, tz - tz_high], axis=0).astype(jnp.bfloat16)
        inner = jnp.dot(lhs, rhs, preferred_element_type=jnp.float32)
        for s in range(species):
            total = [None, None]
            for g, (i, upper) in enumerate(GROUPS):
                r = s * ROWS + 8 * g
                term = inner[r : r + 8] * tx[i : i + 1]
                total[upper] = term if total[upper] is None else total[upper] + term
            summed = total[0] * ty[0:8] + total[1] * ty[8:16]
            gathered[me_sp, s, pl.ds(b, 1), :] = jnp.sum(summed, axis=0, keepdims=True)

    step = count // pieces

    def part_of(slot, k):
        return gathered.at[slot, :, step * k : step * (k + 1), :]

    for k in range(pieces):

        def several(c, carry, k=k):
            for u in range(4):
                block(step * k + 4 * c + u)
            return carry

        lax.fori_loop(0, step // 4, several, 0)
        mine = part_of(me_sp, k)
        for p in range(1, n_sp):
            copies.append(
                remote(mine, mine, sp_send.at[k, p], sp_recv.at[k, p], "sp", sp_ahead[p])
            )
            copies[-1].start()

    loads[3].wait()
    rows_total = species * leaf_dev
    refitted = jnp.zeros((rows_total, width), jnp.float32)
    per = step // leaf_dev
    for k in range(pieces):
        for p in range(1, n_sp):
            there = part_of(sp_behind[p], k)
            remote(there, there, sp_send.at[k, p], sp_recv.at[k, p], "sp", sp_ahead[p]).wait_recv()
        by_species = []
        for s in range(species):
            mixing = jnp.zeros((step, PB), jnp.float32)
            for r in range(n_sp * species):
                other = gathered[r // species, r % species, step * k : step * (k + 1), :]
                mixing = mixing + reaction[me_sp * species + s, r] * other
            by_species.append(
                gathered[me_sp, s, step * k : step * (k + 1), :] + jnp.tanh(mixing)
            )
        reacted = jnp.concatenate(
            [
                jnp.concatenate(
                    [x[m * leaf_dev : (m + 1) * leaf_dev] for x in by_species], axis=0
                )
                for m in range(per)
            ],
            axis=1,
        )
        high, low = split(reacted)
        nodes = slice(k * per * PB, (k + 1) * per * PB)
        main = last_dims(jnp.concatenate([high, low], axis=0), fit_high[:, nodes])
        rest = last_dims(high, fit_low[:, nodes])
        refitted = refitted + (main[:rows_total] + (main[rows_total:] + rest))
    rounded = refitted.astype(jnp.bfloat16)
    half_leaf = leaf_dev // 2
    for s in range(species):
        for h in range(2):
            first = s * leaf_dev + h * half_leaf
            ghosts[h, s] = refitted[first : first + half_leaf].astype(jnp.bfloat16)
    rise = remote(ghosts.at[1], before, ex_send.at[0], ex_recv.at[0], "seg", ahead[1])
    fall = remote(ghosts.at[0], after, ex_send.at[n], ex_recv.at[n], "seg", behind[1])
    loads[7].wait()
    everyone[me] = last_dims(rounded, up[...]).astype(jnp.bfloat16)
    for p in range(1, n):
        mine = everyone.at[me]
        copies.append(remote(mine, mine, ex_send.at[p], ex_recv.at[p], "seg", ahead[p]))
        copies[-1].start()
    rise.start()
    fall.start()

    near_ops, far_ops = near_mat.shape[0], trans.shape[0]
    slot_count = out.shape[1]
    loads[6].wait()
    loads[8].wait()
    loads[9].wait()
    rise.wait()
    fall.wait()
    own_term, highs, lows = [], [], []
    for s in range(species):
        nearby = jnp.concatenate(
            [x.astype(jnp.float32) for x in (before[s], ghosts[0, s], ghosts[1, s], after[s])],
            axis=0,
        ).astype(jnp.bfloat16)
        grouped = jnp.dot(weights[...], nearby, preferred_element_type=jnp.float32)
        own_term.append(grouped[:slot_count])
        high, low = split(grouped[slot_count:])
        highs.append(high)
        lows.append(low)
    total = jnp.concatenate(own_term, axis=0)
    for o in range(near_ops):
        part = slice(o * slot_count, (o + 1) * slot_count)
        stacked = jnp.concatenate(
            [x[part].astype(jnp.float32) for x in highs + lows], axis=0
        ).astype(jnp.bfloat16)
        product = jnp.dot(stacked, near_mat[o], preferred_element_type=jnp.float32)
        total = total + (product[: species * slot_count] + product[species * slot_count :])
    for p in range(1, n):
        there = everyone.at[behind[p]]
        remote(there, there, ex_send.at[p], ex_recv.at[p], "seg", ahead[p]).wait_recv()
    far_rows = []
    for s in range(species):
        source = jnp.concatenate(
            [everyone[e, s * leaf_dev : (s + 1) * leaf_dev, :] for e in range(n)], axis=0
        )
        far_rows.append(jnp.dot(picks[...], source, preferred_element_type=jnp.float32))
    expansion = jnp.zeros((species * slot_count, trans.shape[2]), jnp.float32)
    for o in range(far_ops):
        rows_o = jnp.concatenate(
            [x[o * slot_count : (o + 1) * slot_count] for x in far_rows], axis=0
        ).astype(jnp.bfloat16)
        expansion = expansion + jnp.dot(rows_o, trans[o], preferred_element_type=jnp.float32)
    total = total + jnp.dot(
        expansion.astype(jnp.bfloat16), down[...], preferred_element_type=jnp.float32
    )
    live = table[pl.ds(pl.multiple_of(me * leaf_dev, 8), slot_count), 0:1] == me
    for s in range(species):
        out[s] = jnp.where(live, total[s * slot_count : (s + 1) * slot_count], 0.0)
    for copy in copies:
        copy.wait_send()
    for p in range(1, half):
        there = slots.at[behind[2 * p]]
        remote(there, there, send.at[half + p], recv.at[half + p], "seg", partner).wait_send()


def whole_step(
    coeffs, points, owner_leaf, reaction, fit_matrix, table, near_mat, up_mat, trans_mat,
    down_mat, near_count, far_count,
):
    species, leaf_dev, width = coeffs.shape
    n, n_sp = lax.axis_size("seg"), lax.axis_size("sp")
    blocks = owner_leaf.shape[0]
    count = leaf_dev * blocks
    slots = leaf_dev + 2 * MOVE
    seen = leaf_dev + 2 * (MOVE + REACH)
    half = leaf_dev // 2
    pieces = 3
    f32, bf16, i32 = jnp.float32, jnp.bfloat16, jnp.int32
    dma = pltpu.SemaphoreType.DMA
    return pl.pallas_call(
        functools.partial(step_kernel, n, n_sp, pieces, near_count, far_count),
        out_shape=jax.ShapeDtypeStruct((species, slots, width), f32),
        in_specs=[ANY] * 10,
        out_specs=VMEM,
        scratch_shapes=[
            pltpu.VMEM((n,) + coeffs.shape, f32),
            pltpu.VMEM(points.shape, f32),
            pltpu.SMEM(owner_leaf.shape, i32),
            pltpu.SMEM(reaction.shape, f32),
            pltpu.VMEM(fit_matrix.shape, f32),
            pltpu.VMEM(table.shape, i32),
            pltpu.VMEM(near_mat.shape, bf16),
            pltpu.VMEM(up_mat.shape, bf16),
            pltpu.VMEM(trans_mat.shape, bf16),
            pltpu.VMEM(down_mat.shape, bf16),
            pltpu.VMEM((n * leaf_dev, species * ROWS, 128), f32),
            pltpu.VMEM((3, 16 * count, PB), f32),
            pltpu.VMEM(fit_matrix.shape, bf16),
            pltpu.VMEM(fit_matrix.shape, bf16),
            pltpu.VMEM((n_sp, species, count, PB), f32),
            pltpu.VMEM((2, species, half, width), bf16),
            pltpu.VMEM((species, half, width), bf16),
            pltpu.VMEM((species, half, width), bf16),
            pltpu.VMEM((n, species * leaf_dev, up_mat.shape[0]), bf16),
            pltpu.VMEM(((1 + near_mat.shape[0]) * slots, seen), bf16),
            pltpu.VMEM((far_count * slots, n * leaf_dev), bf16),
            dma((10,)), dma((n,)), dma((n,)), dma((pieces, n_sp)), dma((pieces, n_sp)),
            dma((n + 1,)), dma((n + 1,)),
        ],
        compiler_params=pltpu.CompilerParams(
            collective_id=3, has_side_effects=True, vmem_limit_bytes=LIMIT
        ),
        name="step",
    )(
        coeffs, points, owner_leaf, reaction, fit_matrix, table, near_mat, up_mat, trans_mat,
        down_mat,
    )


def shards(
    coeffs, points, owner_leaf, reaction, fit_matrix, new_seg, near_src, near_op,
    near_mat, up_mat, far_src, trans_mat, down_mat,
):
    species, leaf_dev, width = coeffs.shape
    n = lax.axis_size("seg")
    blocks = owner_leaf.shape[1]
    count = leaf_dev * blocks
    padded_width = -(-width // 128) * 128
    slots = leaf_dev + 2 * MOVE
    table = jnp.concatenate([new_seg[:, None], near_src, near_op, far_src], axis=1)
    table = jnp.pad(table, ((MOVE, MOVE), (0, 0)), constant_values=-1)
    if n * leaf_dev * species * ROWS * 512 <= LIMIT // 2:
        return whole_step(
            coeffs, points, owner_leaf.T, reaction, fit_matrix.T, table, near_mat, up_mat.T,
            trans_mat, down_mat, near_src.shape[1], far_src.shape[1],
        )
    mine = jnp.transpose(coeffs, (1, 0, 2))
    everyone = pair_gather(mine, "seg", 0).reshape(n * leaf_dev, species, width)
    values = pl.pallas_call(
        evaluate_kernel,
        out_shape=jax.ShapeDtypeStruct((species, count, PB), jnp.float32),
        in_specs=[SMEM, VMEM, VMEM],
        out_specs=VMEM,
        scratch_shapes=[
            pltpu.VMEM((8, padded_width), jnp.float32),
            pltpu.VMEM((count * species * ROWS, 128), jnp.float32),
            pltpu.VMEM((3, 16 * count, PB), jnp.float32),
        ],
        compiler_params=pltpu.CompilerParams(vmem_limit_bytes=LIMIT),
        name="evaluate",
    )(owner_leaf, everyone, points)
    gathered = pair_gather(values, "sp", 1)
    half = leaf_dev // 2
    ghosts, equivalent = pl.pallas_call(
        refit_kernel,
        out_shape=(
            jax.ShapeDtypeStruct((2, species, half, width), jnp.bfloat16),
            jax.ShapeDtypeStruct((species * leaf_dev, up_mat.shape[1]), jnp.bfloat16),
        ),
        in_specs=[SMEM, VMEM, VMEM, VMEM, VMEM],
        out_specs=(VMEM, VMEM),
        scratch_shapes=[pltpu.VMEM((species * leaf_dev, blocks * PB), jnp.float32)],
        compiler_params=pltpu.CompilerParams(vmem_limit_bytes=LIMIT),
        name="refit",
    )(reaction, values, gathered, fit_matrix, up_mat)
    before, after, all_equivalent = pl.pallas_call(
        functools.partial(exchange_kernel, n),
        out_shape=(
            jax.ShapeDtypeStruct((species, half, width), jnp.bfloat16),
            jax.ShapeDtypeStruct((species, half, width), jnp.bfloat16),
            jax.ShapeDtypeStruct((n,) + equivalent.shape, jnp.bfloat16),
        ),
        in_specs=[ANY, ANY],
        out_specs=(ANY, ANY, ANY),
        scratch_shapes=[
            pltpu.SemaphoreType.DMA((n + 1,)),
            pltpu.SemaphoreType.DMA((n + 1,)),
            pltpu.SemaphoreType.DMA,
        ],
        compiler_params=pltpu.CompilerParams(collective_id=2, has_side_effects=True),
        name="exchange",
    )(ghosts, equivalent)
    return pl.pallas_call(
        functools.partial(
            finish_kernel, near_count=near_src.shape[1], far_count=far_src.shape[1]
        ),
        out_shape=jax.ShapeDtypeStruct((species, slots, width), jnp.float32),
        in_specs=[VMEM] * 8,
        out_specs=VMEM,
        compiler_params=pltpu.CompilerParams(vmem_limit_bytes=LIMIT),
        name="finish",
    )(table, ghosts, before, after, all_equivalent, near_mat, trans_mat, down_mat)


def solution(mesh):
    placed = (P("sp", "seg", None), P(None, "seg", None), P("seg", None)) + (P(),) * 10
    return jax.shard_map(
        shards, mesh=mesh, in_specs=placed, out_specs=P("sp", "seg", None), check_vma=False
    )
```
